32 devices in a mesh: visit: 8 (over y, x, core), quad: 4 (over z).
Axes of the slice: x: 2, y: 2, z: 4, core: 2. Of those that a mesh axis runs over, the one named last changes fastest.
Arguments:
- template: float32 [6, 128, 256], P(None, 'quad', 'visit'), may hold values from -8 to 8
- science: float32 [8, 128, 256], P('visit', 'quad'), may hold values from -8 to 8
- variance: float32 [8, 128, 256], P('visit', 'quad'), may hold values from 0.5 to 2
- coeffs: float32 [8, 31, 6], P('visit'), may hold values from -3 to 3
- visit_weight: float32 [8], P('visit'), may hold values from 0.3 to 1
- band: int32 [8], P('visit'), may hold values from 0 to 5
- footprint: int32 [8, 8, 16], P('visit', 'quad'), may hold values 0 or 1
Outputs:
- coadd: float32 [6, 128, 256], P(None, 'quad', 'visit')
The draws below stay inside these ranges and needn't reach their ends.
Inputs may be any that keep to these rules, and one draw needn't show every extreme that they name: `footprint`: 0 or 1 for each tile.
All inputs are finite; a program needn't handle non-finite values. No bound on the sum of `footprint` on one device may be relied on, other than what follows from the above.
Results may differ from the reference program's by a relative error of at most 0.0003.
Values sent between devices are 32-bit elements; how exact they have to be, the bound alone decides.
No kernel may reach another device: no remote copies, remote signals or barrier semaphores. Data moves between devices by JAX's collectives and lax.ppermute only.
A program may use at most 128 MiB of HBM per device.

```python
import math
import jax
import jax.numpy as jnp
from jax import lax

B = 6
RAD = 10
NB = 31
NP = 6
TILE = 16
ROWS = 128
COLS = 256
VISITS = 8


def with_ends(entries, key, least, largest):
    index_at = [jax.random.randint(jax.random.fold_in(key, axis), (), 0, length) for axis, length in enumerate(entries.shape)]
    widest = entries.shape.index(max(entries.shape))
    beside = index_at[:widest] + [(index_at[widest] + 1) % entries.shape[widest]] + index_at[widest + 1:]
    return entries.at[tuple(index_at)].set(least).at[tuple(beside)].set(largest)


def shard_levels(own_key, extent, shards, smallest, top_value):
    def one(dim, blocks):
        steps = jax.random.uniform(jax.random.fold_in(jax.random.fold_in(own_key, 6), dim), (blocks,), jnp.float32, smallest / len(shards), top_value / len(shards))
        return jnp.repeat(jnp.exp(steps), extent[dim] // blocks).reshape((-1,) + (1,) * (len(extent) - dim - 1))

    level = one(*shards[0])
    for cut in shards[1:]:
        level = level * one(*cut)
    return level


def normal_values(rng, extent, scale, most, cuts=(), held_as=jnp.bfloat16):
    factor_of = shard_levels(rng, extent, cuts, -0.22, 0.18) if cuts else 1.0
    drawn = jax.random.normal(rng, extent, jnp.float32) * scale * factor_of
    return jnp.minimum(jnp.maximum(drawn, -most), most).astype(held_as)


def setup_inputs(seed: int = 0) -> dict:
    key_of = jax.random.split(jax.random.key(seed), 8)
    template = normal_values(key_of[0], (B, ROWS, COLS), 1.0, 8.0, ((1, 4), (2, 8)), jnp.float32)
    science = normal_values(key_of[1], (VISITS, ROWS, COLS), 1.0, 8.0, ((0, 8), (1, 4)), jnp.float32)
    variance = jnp.clip(jnp.exp(math.log(2.0) - 1.3862944 * jax.random.uniform(key_of[2], (VISITS, ROWS, COLS), jnp.float32) ** shard_levels(key_of[2], (VISITS, ROWS, COLS), ((0, 8), (1, 4)), -0.2, 0.2)), 0.5, 2.0)
    coeffs = normal_values(key_of[3], (VISITS, NB, NP), 0.5, 3.0, ((0, 8),), jnp.float32)
    visit_weight = jnp.clip(jnp.exp(math.log(1.0) - 1.2039728 * jax.random.uniform(key_of[4], (VISITS,), jnp.float32) ** shard_levels(key_of[4], (VISITS,), ((0, 8),), -0.2, 0.2)), 0.3, 1.0)
    band = with_ends(jax.random.randint(key_of[5], (VISITS,), 0, B), jax.random.fold_in(key_of[5], 1), 0, B - 1).astype(jnp.int32)
    footprint = with_ends((jax.random.randint(key_of[6], (VISITS, ROWS // TILE, COLS // TILE), 0, 4) < 3).astype(jnp.int32), jax.random.fold_in(key_of[6], 1), 0, 1)
    return dict(template=template, science=science, variance=variance, coeffs=coeffs, visit_weight=visit_weight, band=band, footprint=footprint)


SIGMAS = (1.0, 2.5, 5.0)
DEGREES = (4, 3, 2)


def filter_taps(sigma, power, radius):
    offsets = jnp.arange(-radius, radius + 1).astype(jnp.float32)
    bell = jnp.exp(-offsets * offsets / (2.0 * sigma * sigma))
    return bell / jnp.sum(bell) * (offsets / sigma) ** power


def row_table(taps, out_rows, radius):
    outs = jnp.arange(out_rows)[:, None]
    inputs = jnp.arange(out_rows + 2 * radius)[None, :]
    offset = inputs - outs
    hits = (offset[:, :, None] == jnp.arange(2 * radius + 1)[None, None, :]).astype(jnp.float32)
    return jnp.sum(hits * taps, axis=-1)


def reference(template, science, variance, coeffs, visit_weight, band, footprint):
    column_filters = []
    for gauss in range(3):
        for power in range(DEGREES[gauss] + 1):
            column_filters.append(filter_taps(SIGMAS[gauss], power, RAD))
    kernel = jnp.stack(column_filters)[:, None, None, :]
    xcoord = ((jnp.arange(COLS).astype(jnp.float32) + 0.5) / COLS * 2.0 - 1.0)[None, :]
    ycoord = ((jnp.arange(ROWS).astype(jnp.float32) + 0.5) / ROWS * 2.0 - 1.0)[:, None]
    polys = [jnp.ones_like(xcoord * ycoord), xcoord + 0.0 * ycoord, ycoord + 0.0 * xcoord,
             xcoord * xcoord + 0.0 * ycoord, xcoord * ycoord, ycoord * ycoord + 0.0 * xcoord]

    def one_visit(total, items):
        sci, var, coef, weight, which, foot = items
        image = lax.dynamic_index_in_dim(template, which, 0, keepdims=False)
        extended = jnp.pad(image, ((RAD, RAD), (0, 0)))
        colconv = lax.conv_general_dilated(extended[None, None], kernel, (1, 1), ((0, 0), (RAD, RAD)),
                                           precision=lax.Precision.HIGHEST)[0]
        model = jnp.zeros((ROWS, COLS), jnp.float32)
        basis = 0
        start = 0
        for gauss in range(3):
            degree = DEGREES[gauss]
            for row_power in range(degree + 1):
                table = row_table(filter_taps(SIGMAS[gauss], row_power, RAD), ROWS, RAD)
                for col_power in range(degree + 1 - row_power):
                    conv = jnp.dot(table, colconv[start + col_power], precision=lax.Precision.HIGHEST,
                                   preferred_element_type=jnp.float32)
                    spatial = coef[basis, 0] * polys[0]
                    for term_index in range(1, NP):
                        spatial = spatial + coef[basis, term_index] * polys[term_index]
                    model = model + spatial * conv
                    basis += 1
            start += degree + 1
        cover = jnp.repeat(jnp.repeat(foot, TILE, 0), TILE, 1).astype(jnp.float32)
        term = weight * cover * (sci - model) / var
        onehot = (jnp.arange(B) == which).astype(jnp.float32)
        return total + onehot[:, None, None] * term[None], None

    start_total = jnp.zeros((B, ROWS, COLS), jnp.float32)
    coadd, unused = lax.scan(one_visit, start_total,
                             (science, variance, coeffs, visit_weight, band, footprint))
    return coadd
```

```python
import math

import jax
import jax.numpy as jnp
import numpy as np
from jax import lax
from jax.experimental import pallas as pl
from jax.experimental.pallas import tpu as pltpu
from jax.sharding import PartitionSpec as P

RAD = 10
EDGE = 16
SIGMAS = (1.0, 2.5, 5.0)
DEGREES = (4, 3, 2)
GROUP = 4
F32 = jnp.float32
BF16 = jnp.bfloat16


def taps(sigma, power):
    offsets = np.arange(-RAD, RAD + 1).astype(np.float64)
    bell = np.exp(-offsets * offsets / (2.0 * sigma * sigma))
    return bell / bell.sum() * (offsets / sigma) ** power


def band_matrix(positions, outs):
    tables = []
    for sigma, degree in zip(SIGMAS, DEGREES):
        for power in range(degree + 1):
            filt = taps(sigma, power)
            offset = positions[None, :] - np.arange(outs)[:, None]
            inside = np.abs(offset) <= RAD
            tables.append(np.where(inside, filt[np.clip(offset + RAD, 0, 2 * RAD)], 0.0))
    return np.stack(tables).astype(np.float32)


def split(array):
    high = array.astype(BF16)
    low = (array.astype(F32) - high.astype(F32)).astype(BF16)
    return high, low


def np_split(array):
    high = array.astype(jnp.bfloat16)
    low = (array - high.astype(np.float32)).astype(jnp.bfloat16)
    return high, low


def row_weights(rows):
    positions = np.concatenate(
        [np.arange(rows), np.arange(EDGE) - EDGE, rows + np.arange(EDGE)]
    )
    table = band_matrix(positions, rows).reshape(-1, rows + 2 * EDGE)
    high, low = np_split(table)
    return np.concatenate([high, high, low], axis=1)


def column_weights(cols, lanes):
    far = 10 * cols + 1000
    positions = np.concatenate(
        [
            np.arange(cols),
            np.arange(RAD) - RAD,
            cols + np.arange(RAD),
            np.full(lanes - cols - 2 * RAD, far),
        ]
    )
    table = band_matrix(positions, cols)
    count = table.shape[0]
    wide = np.zeros((GROUP, lanes, count, GROUP, cols), np.float32)
    for v in range(GROUP):
        wide[v, :, :, v, :] = table.transpose(2, 0, 1)
    return np_split(wide.reshape(GROUP * lanes, count * GROUP * cols))


def pack_kernel(
    visits, t_ref, n_ref, s_ref, sci_ref, var_ref, coef_ref, foot_ref, w_ref, band_ref, out_ref, own
):
    bands, rows, cols = t_ref.shape
    ext = rows + 2 * EDGE
    me = lax.axis_index("visit")
    lane = lax.broadcasted_iota(jnp.int32, (ext, 128), 1)
    for b in range(bands):
        own[b, 0:rows, 0:cols] = t_ref[b]
        own[b, rows : rows + EDGE, 0:cols] = n_ref[b]
        own[b, rows + EDGE : ext, 0:cols] = s_ref[b]
    left = jnp.zeros((ext, 128), F32)
    right = jnp.zeros((ext, 128), F32)
    for b in range(bands):
        tile = own[b]
        at = 64 + RAD * b
        here = (lane >= at) & (lane < at + RAD)
        left = jnp.where(here, pltpu.roll(tile, at, 1), left)
        right = jnp.where(here, pltpu.roll(tile, (at - (cols - RAD)) % 128, 1), right)
    weight = w_ref[0]
    tile_rows, tile_cols = foot_ref.shape[1], foot_ref.shape[2]
    foot = foot_ref[0].astype(F32)
    width = sci_ref.shape[2]
    side = rows // tile_rows
    span = width // tile_cols
    per = 128 // span
    tcol = lax.broadcasted_iota(jnp.int32, (tile_cols, 128), 0)
    tlane = lax.broadcasted_iota(jnp.int32, (tile_cols, 128), 1) // span
    band_value = band_ref[0].astype(F32)
    parts = []
    for chunk in range(width // 128):
        pick = jnp.where(tcol == tlane + chunk * per, 1.0, 0.0).astype(F32)
        cover = jnp.dot(foot, pick, preferred_element_type=F32)
        cover = jnp.concatenate(
            [jnp.broadcast_to(cover[k : k + 1], (side, 128)) for k in range(tile_rows)], axis=0
        )
        at = slice(chunk * 128, chunk * 128 + 128)
        scale = weight * cover / var_ref[0, :, at]
        parts.append((scale * sci_ref[0, :, at], scale))
    top = lane[:rows]
    zero = jnp.zeros((ext - rows, 128), F32)
    for d in range(visits):
        whole, inner = (d * cols) // 128, (d * cols) % 128
        first, second = parts[whole]
        pair = jnp.where(
            top < 32,
            pltpu.roll(first, (128 - inner) % 128, 1),
            pltpu.roll(second, (160 - inner) % 128, 1),
        )
        edge = jnp.where(d < me, left, right)
        out_ref[d] = jnp.where(lane < 64, jnp.concatenate([pair, zero], axis=0), edge)
        out_ref[d, rows : rows + coef_ref.shape[1], 0 : coef_ref.shape[2]] = coef_ref[0]
        out_ref[d, ext - 1 : ext, 0:64] = jnp.full((1, 64), band_value, F32)


def model_kernel(
    visits, quads, g_ref, t_ref, n_ref, s_ref, tab_ref, dh_ref, dl_ref, out_ref, own, acc
):
    bands, rows, cols = t_ref.shape
    ext = rows + 2 * EDGE
    width = visits * cols
    total = quads * rows
    me = lax.axis_index("visit")
    quad = lax.axis_index("quad")
    lane = lax.broadcasted_iota(jnp.int32, (ext, 128), 1)
    for b in range(bands):
        own[b, 0:rows, 0:cols] = t_ref[b]
        own[b, rows : rows + EDGE, 0:cols] = n_ref[b]
        own[b, rows + EDGE : ext, 0:cols] = s_ref[b]
    west = jnp.where(me > 0, g_ref[jnp.maximum(me - 1, 0)], 0.0)
    east = jnp.where(me < visits - 1, g_ref[jnp.minimum(me + 1, visits - 1)], 0.0)
    for b in range(bands):
        at = 64 + RAD * b
        tile = jnp.where(
            lane < cols,
            own[b],
            jnp.where(
                lane < cols + RAD,
                pltpu.roll(west, (cols - at) % 128, 1),
                jnp.where(
                    lane < cols + 2 * RAD, pltpu.roll(east, (cols + RAD - at) % 128, 1), 0.0
                ),
            ),
        )
        own[b] = jnp.where(lane < 64, tile, pltpu.roll(tile, 64, 1))
    tlane = lax.broadcasted_iota(jnp.int32, (rows, 128), 1)
    trow = lax.broadcasted_iota(jnp.int32, (rows, 128), 0)
    x = (((tlane % cols) + me * cols).astype(F32) + 0.5) / width * 2.0 - 1.0
    y = ((trow + quad * rows).astype(F32) + 0.5) / total * 2.0 - 1.0
    yy = y * y
    acc[...] = jnp.zeros_like(acc)

    def group(start):
        band_rows = [g_ref[start + v, ext - 1 : ext, :] for v in range(GROUP)]
        pairs = []
        for p in range(GROUP // 2):
            which = jnp.where(
                lane[:1] < 64, band_rows[2 * p], pltpu.roll(band_rows[2 * p + 1], 64, 1)
            )
            which = jnp.broadcast_to(which, (ext, 128))
            tile = jnp.zeros((ext, 128), F32)
            for b in range(bands):
                tile = jnp.where(which == float(b), own[b], tile)
            pairs.append(tile)
        high, low = split(jnp.concatenate(pairs, axis=1))
        rowed = jnp.dot(
            tab_ref[...], jnp.concatenate([high, low, high], axis=0), preferred_element_type=F32
        )
        rhigh, rlow = split(rowed)
        cmat = jnp.zeros((rows, 128), F32)
        first = jnp.zeros((rows, 128), F32)
        second = jnp.zeros((rows, 128), F32)
        which = jnp.zeros((1, 128), F32)
        for v in range(GROUP):
            here = (tlane >= v * cols) & (tlane < (v + 1) * cols)
            block = g_ref[start + v, 0:rows, :]
            coef = g_ref[start + v, rows : 2 * rows, :]
            first = jnp.where(here, pltpu.roll(block, v * cols, 1), first)
            second = jnp.where(here, pltpu.roll(block, (v * cols - 32) % 128, 1), second)
            cmat = jnp.where(here, pltpu.roll(coef, v * cols, 1), cmat)
            turned = band_rows[v] if v < 2 else pltpu.roll(band_rows[v], 64, 1)
            which = jnp.where(here[:1], turned, which)
        base = tlane - tlane % cols
        terms = [jnp.take_along_axis(cmat, base + s, axis=1) for s in range(6)]
        poly0 = terms[0] + x * (terms[1] + x * terms[3])
        poly1 = terms[2] + x * terms[4]
        poly2 = terms[5]
        model = jnp.zeros((rows, 128), F32)
        basis_start = 0
        filt = 0
        for degree in DEGREES:
            count = degree + 1
            index = {}
            k = basis_start
            for i in range(count):
                for j in range(count - i):
                    index[i, j] = k
                    k += 1
            for j0 in range(0, count, 2):
                js = range(j0, min(j0 + 2, count))
                tall = (count - j0) * rows
                at = slice((filt + j0) * 128, (filt + js[-1] + 1) * 128)
                dh, dl = dh_ref[:, at], dl_ref[:, at]
                rh = rhigh[filt * rows : filt * rows + tall]
                rl = rlow[filt * rows : filt * rows + tall]
                conv = (
                    jnp.dot(rh, dh, preferred_element_type=F32)
                    + jnp.dot(rl, dh, preferred_element_type=F32)
                    + jnp.dot(rh, dl, preferred_element_type=F32)
                )
                for j in js:
                    for i in range(count - j):
                        n = index[i, j]
                        part = conv[i * rows : (i + 1) * rows, (j - j0) * 128 : (j - j0 + 1) * 128]
                        spatial = (
                            poly0[n : n + 1] + y * poly1[n : n + 1] + yy * poly2[n : n + 1]
                        )
                        model = model + spatial * part
            basis_start = k
            filt += count
        term = first - second * model
        which = jnp.broadcast_to(which, (rows, 128))
        for b in range(bands):
            acc[b] += jnp.where(which == float(b), term, 0.0)

    if visits // GROUP <= 2:
        for g in range(visits // GROUP):
            group(g * GROUP)
    else:

        @pl.loop(0, visits // GROUP)
        def _(g):
            group(g * GROUP)

    for b in range(bands):
        half = acc[b] + pltpu.roll(acc[b], 64, 1)
        out_ref[b] = (half + pltpu.roll(half, 96, 1))[:, 0:cols]


def per_device(template, science, variance, coeffs, visit_weight, band, footprint):
    visits, quads = lax.axis_size("visit"), lax.axis_size("quad")
    bands, rows, cols = template.shape
    ext = rows + 2 * EDGE
    up = [(i, i + 1) for i in range(quads - 1)]
    down = [(i + 1, i) for i in range(quads - 1)]
    north = lax.ppermute(template[:, rows - EDGE :], "quad", up)
    south = lax.ppermute(template[:, :EDGE], "quad", down)
    vmem = pl.BlockSpec(memory_space=pltpu.VMEM)
    smem = pl.BlockSpec(memory_space=pltpu.SMEM)

    def packing(*refs):
        pack_kernel(visits, *refs)

    def modelling(*refs):
        model_kernel(visits, quads, *refs)

    blocks = pl.pallas_call(
        packing,
        out_shape=jax.ShapeDtypeStruct((visits, ext, 128), F32),
        in_specs=[vmem] * 7 + [smem] * 2,
        out_specs=vmem,
        scratch_shapes=[pltpu.VMEM((bands, ext, 128), F32)],
        name="pack",
    )(template, north, south, science, variance, coeffs, footprint, visit_weight, band)
    gathered = lax.all_to_all(blocks, "visit", 0, 0, tiled=True)
    table = jnp.asarray(row_weights(rows))
    dh, dl = column_weights(cols, 64)
    return pl.pallas_call(
        modelling,
        out_shape=jax.ShapeDtypeStruct((bands, rows, cols), F32),
        in_specs=[vmem] * 7,
        out_specs=vmem,
        scratch_shapes=[
            pltpu.VMEM((bands, ext, 128), F32),
            pltpu.VMEM((bands, rows, 128), F32),
        ],
        name="model",
    )(gathered, template, north, south, table, jnp.asarray(dh), jnp.asarray(dl))


def solution(mesh):
    placed = (
        P(None, "quad", "visit"),
        P("visit", "quad", None),
        P("visit", "quad", None),
        P("visit", None, None),
        P("visit"),
        P("visit"),
        P("visit", "quad", None),
    )
    return jax.shard_map(
        per_device, mesh=mesh, in_specs=placed, out_specs=P(None, "quad", "visit"), check_vma=False
    )
```

```python
import jax
import jax.numpy as jnp
import numpy as np
from jax import lax
from jax.experimental import pallas as pl
from jax.experimental.pallas import tpu as pltpu
from jax.sharding import PartitionSpec as P


RAD = 10
EDGE = 16
SIGMAS = (1.0, 2.5, 5.0)
DEGREES = (4, 3, 2)
GROUP = 4
F32 = jnp.float32
BF16 = jnp.bfloat16


def taps(sigma, power):
    offsets = np.arange(-RAD, RAD + 1).astype(np.float64)
    bell = np.exp(-offsets * offsets / (2.0 * sigma * sigma))
    return bell / bell.sum() * (offsets / sigma) ** power


def band_matrix(positions, outs):
    tables = []
    for sigma, degree in zip(SIGMAS, DEGREES):
        for power in range(degree + 1):
            filt = taps(sigma, power)
            offset = positions[None, :] - np.arange(outs)[:, None]
            inside = np.abs(offset) <= RAD
            tables.append(np.where(inside, filt[np.clip(offset + RAD, 0, 2 * RAD)], 0.0))
    return np.stack(tables).astype(np.float32)


def split(array):
    high = array.astype(BF16)
    low = (array.astype(F32) - high.astype(F32)).astype(BF16)
    return high, low


def np_split(array):
    high = array.astype(jnp.bfloat16)
    low = (array - high.astype(np.float32)).astype(jnp.bfloat16)
    return high, low


def row_weights(rows):
    positions = np.concatenate(
        [np.arange(rows), np.arange(EDGE) - EDGE, rows + np.arange(EDGE)]
    )
    table = band_matrix(positions, rows).reshape(-1, rows + 2 * EDGE)
    high, low = np_split(table)
    return np.concatenate([high, high, low], axis=1)


def column_weights(cols, lanes):
    far = 10 * cols + 1000
    positions = np.concatenate(
        [
            np.arange(cols),
            np.arange(RAD) - RAD,
            cols + np.arange(RAD),
            np.full(lanes - cols - 2 * RAD, far),
        ]
    )
    table = band_matrix(positions, cols)
    count = table.shape[0]
    wide = np.zeros((GROUP, lanes, count, GROUP, cols), np.float32)
    for v in range(GROUP):
        wide[v, :, :, v, :] = table.transpose(2, 0, 1)
    return np_split(wide.reshape(GROUP * lanes, count * GROUP * cols))


def lanes_of(shape):
    return lax.broadcasted_iota(jnp.int32, shape, 1)


def load_kernel(count, *refs):
    sources, core_ref, other_ref = refs[:count], refs[count], refs[count + 1]
    targets, sems, tile_ref = refs[count + 2 : -2], refs[-2], refs[-1]
    copies = [
        pltpu.make_async_copy(a, b, sems.at[i]) for i, (a, b) in enumerate(zip(sources, targets))
    ]
    for copy in copies:
        copy.start()
    for copy in copies:
        copy.wait()
    t_ref = targets[0]
    bands, rows, cols = t_ref.shape
    lane = lanes_of((rows, 128))
    left = jnp.zeros((rows, 128), F32)
    right = jnp.zeros((rows, 128), F32)
    for b in range(bands):
        tile_ref[0:rows, 0:cols] = t_ref[b]
        tile = tile_ref[...]
        at = RAD * b
        here = (lane >= at) & (lane < at + RAD)
        left = jnp.where(here, pltpu.roll(tile, at, 1), left)
        right = jnp.where(here, pltpu.roll(tile, (at - (cols - RAD)) % 128, 1), right)
    even = lax.axis_index("visit") % 2 == 0
    core_ref[...] = jnp.where(even, right, left)
    other_ref[...] = jnp.where(even, left, right)


def pack_kernel(visits, cols, sci_ref, var_ref, coef_ref, foot_ref, meta_ref, out_ref):
    rows = sci_ref.shape[1]
    lane = lanes_of((rows, 128))
    weight = jnp.broadcast_to(meta_ref[:, 0:1], (rows, 128))
    which = jnp.broadcast_to(meta_ref[:, 1:2], (1, 64))
    tile_rows, tile_cols = foot_ref.shape[1], foot_ref.shape[2]
    foot = foot_ref[0].astype(F32)
    width = sci_ref.shape[2]
    side = rows // tile_rows
    span = width // tile_cols
    per = 128 // span
    tcol = lax.broadcasted_iota(jnp.int32, (tile_cols, 128), 0)
    tlane = lanes_of((tile_cols, 128)) // span
    parts = []
    for chunk in range(width // 128):
        pick = jnp.where(tcol == tlane + chunk * per, 1.0, 0.0).astype(F32)
        cover = jnp.dot(foot, pick, preferred_element_type=F32)
        cover = jnp.concatenate(
            [jnp.broadcast_to(cover[k : k + 1], (side, 128)) for k in range(tile_rows)], axis=0
        )
        at = slice(chunk * 128, chunk * 128 + 128)
        scale = weight * cover / var_ref[0, :, at]
        parts.append((scale * sci_ref[0, :, at], scale))
    coef = coef_ref[:, 0, :]
    terms, basis = coef.shape
    for d in range(visits):
        whole, inner = (d * cols) // 128, (d * cols) % 128
        first, second = parts[whole]
        out_ref[d] = jnp.where(
            lane < 32,
            pltpu.roll(first, (128 - inner) % 128, 1),
            pltpu.roll(second, (160 - inner) % 128, 1),
        )
        for s in range(terms):
            out_ref[d, s : s + 1, 64 : 64 + basis] = coef[s : s + 1]
        out_ref[d, 8:9, 64:128] = which


def widen_kernel(t_ref, core_ref, other_ref, near_ref, first_ref, second_ref):
    bands, rows, cols = t_ref.shape
    lane = lanes_of((rows, 128))
    even = lax.axis_index("visit") % 2 == 0
    upper = lax.axis_index("quad") % 2 == 0
    core, other = core_ref[...], other_ref[...]
    west = jnp.where(even, other, core)
    east = jnp.where(even, core, other)
    near_ref[:, :, 0:cols] = t_ref[...]
    for b in range(bands):
        at = RAD * b
        tile = jnp.where(
            lane < cols,
            near_ref[b],
            jnp.where(
                lane < cols + RAD,
                pltpu.roll(west, (cols - at) % 128, 1),
                jnp.where(
                    lane < cols + 2 * RAD, pltpu.roll(east, (cols + RAD - at) % 128, 1), 0.0
                ),
            ),
        )
        tile = jnp.where(lane < 64, tile, pltpu.roll(tile, 64, 1))
        near_ref[b] = tile
        last, leading = tile[rows - EDGE :], tile[:EDGE]
        first_ref[b] = jnp.where(upper, last, leading)
        second_ref[b] = jnp.where(upper, leading, last)


def model_kernel(
    visits,
    quads,
    g_ref,
    near_ref,
    a_ref,
    b_ref,
    tab_hbm,
    dh_hbm,
    dl_hbm,
    out_ref,
    own,
    acc,
    tab_ref,
    dh_ref,
    dl_ref,
    sems,
):
    tables = ((tab_hbm, tab_ref), (dh_hbm, dh_ref), (dl_hbm, dl_ref))
    copies = [pltpu.make_async_copy(a, b, sems.at[i]) for i, (a, b) in enumerate(tables)]
    for copy in copies:
        copy.start()
    bands, rows, cols = out_ref.shape
    ext = rows + 2 * EDGE
    width = visits * cols
    total = quads * rows
    me = lax.axis_index("visit")
    quad = lax.axis_index("quad")
    lane = lanes_of((ext, 128))
    upper = quad % 2 == 0
    for b in range(bands):
        own[b, 0:rows] = near_ref[b]
        own[b, rows : rows + EDGE] = jnp.where(upper, b_ref[b], a_ref[b])
        own[b, rows + EDGE : ext] = jnp.where(upper, a_ref[b], b_ref[b])
    tlane = lanes_of((rows, 128))
    trow = lax.broadcasted_iota(jnp.int32, (rows, 128), 0)
    x = (((tlane % cols) + me * cols).astype(F32) + 0.5) / width * 2.0 - 1.0
    y = ((trow + quad * rows).astype(F32) + 0.5) / total * 2.0 - 1.0
    yy = y * y
    acc[...] = jnp.zeros_like(acc)
    for copy in copies:
        copy.wait()

    def group(start):
        high_rows = [g_ref[start + v, 8:9, :] for v in range(GROUP)]
        low_rows = [pltpu.roll(row, 64, 1) for row in high_rows]
        pairs = []
        for p in range(GROUP // 2):
            which = jnp.where(lane[:1] < 64, low_rows[2 * p], high_rows[2 * p + 1])
            which = jnp.broadcast_to(which, (ext, 128))
            tile = jnp.zeros((ext, 128), F32)
            for b in range(bands):
                tile = jnp.where(which == float(b), own[b], tile)
            pairs.append(tile)
        high, low = split(jnp.concatenate(pairs, axis=1))
        rowed = jnp.dot(
            tab_ref[...], jnp.concatenate([high, low, high], axis=0), preferred_element_type=F32
        )
        rhigh, rlow = split(rowed)
        first = jnp.zeros((rows, 128), F32)
        second = jnp.zeros((rows, 128), F32)
        which = jnp.zeros((1, 128), F32)
        packed = []
        for v in range(GROUP):
            here = (tlane >= v * cols) & (tlane < (v + 1) * cols)
            block = g_ref[start + v]
            first = jnp.where(here, pltpu.roll(block, v * cols, 1), first)
            second = jnp.where(here, pltpu.roll(block, (v * cols - 32) % 128, 1), second)
            packed.append(pltpu.roll(block[0:8], 64, 1))
            turned = low_rows[v] if v < 2 else high_rows[v]
            which = jnp.where(here[:1], turned, which)
        packed.append(jnp.zeros((128 - 8 * GROUP, 128), F32))
        cmat = jnp.transpose(jnp.concatenate(packed, axis=0))[0:rows]
        base = 8 * (tlane // cols)
        terms = [jnp.take_along_axis(cmat, base + s, axis=1) for s in range(6)]
        poly0 = terms[0] + x * (terms[1] + x * terms[3])
        poly1 = terms[2] + x * terms[4]
        poly2 = terms[5]
        model = jnp.zeros((rows, 128), F32)
        basis_start = 0
        filt = 0
        for degree in DEGREES:
            count = degree + 1
            index = {}
            k = basis_start
            for i in range(count):
                for j in range(count - i):
                    index[i, j] = k
                    k += 1
            for j0 in range(0, count, 2):
                js = range(j0, min(j0 + 2, count))
                tall = (count - j0) * rows
                at = slice((filt + j0) * 128, (filt + js[-1] + 1) * 128)
                dh, dl = dh_ref[:, at], dl_ref[:, at]
                rh = rhigh[filt * rows : filt * rows + tall]
                rl = rlow[filt * rows : filt * rows + tall]
                conv = (
                    jnp.dot(rh, dh, preferred_element_type=F32)
                    + jnp.dot(rl, dh, preferred_element_type=F32)
                    + jnp.dot(rh, dl, preferred_element_type=F32)
                )
                for j in js:
                    for i in range(count - j):
                        n = index[i, j]
                        part = conv[i * rows : (i + 1) * rows, (j - j0) * 128 : (j - j0 + 1) * 128]
                        spatial = (
                            poly0[n : n + 1] + y * poly1[n : n + 1] + yy * poly2[n : n + 1]
                        )
                        model = model + spatial * part
            basis_start = k
            filt += count
        term = first - second * model
        which = jnp.broadcast_to(which, (rows, 128))
        for b in range(bands):
            acc[b] += jnp.where(which == float(b), term, 0.0)

    if visits // GROUP <= 2:
        for g in range(visits // GROUP):
            group(g * GROUP)
    else:

        @pl.loop(0, visits // GROUP)
        def _(g):
            group(g * GROUP)

    for b in range(bands):
        half = acc[b] + pltpu.roll(acc[b], 64, 1)
        out_ref[b] = (half + pltpu.roll(half, 96, 1))[:, 0:cols]


def swaps(count, start):
    pairs = [(i, i + 1) for i in range(start, count - 1, 2)]
    return pairs + [(j, i) for i, j in pairs]


def stay(array):
    return pltpu.with_memory_space_constraint(array, pltpu.HBM)


def per_device(template, science, variance, coeffs, visit_weight, band, footprint):
    visits, quads = lax.axis_size("visit"), lax.axis_size("quad")
    bands, rows, cols = template.shape
    ext = rows + 2 * EDGE
    vmem = pl.BlockSpec(memory_space=pltpu.VMEM)
    hbm = pl.BlockSpec(memory_space=pltpu.HBM)
    params = pltpu.CompilerParams(vmem_limit_bytes=24 * 1024 * 1024)

    def packing(*refs):
        pack_kernel(visits, cols, *refs)

    def modelling(*refs):
        model_kernel(visits, quads, *refs)

    turned = jnp.transpose(coeffs, (2, 0, 1))
    sources = [stay(array) for array in (template, science, variance, turned, footprint)]
    strip = jax.ShapeDtypeStruct((rows, 128), F32)

    def loading(*refs):
        load_kernel(len(sources), *refs)

    to_core, to_other, tile, *loaded = pl.pallas_call(
        loading,
        out_shape=[strip, strip] + [jax.ShapeDtypeStruct(a.shape, a.dtype) for a in sources],
        in_specs=[hbm] * len(sources),
        out_specs=[vmem] * (2 + len(sources)),
        scratch_shapes=[
            pltpu.SemaphoreType.DMA((len(sources),)),
            pltpu.VMEM((rows, 128), F32),
        ],
        compiler_params=params,
        name="load",
    )(*sources)
    core = lax.ppermute(to_core, "visit", swaps(visits, 0))
    other = lax.ppermute(to_other, "visit", swaps(visits, 1))
    meta = lax.pad(visit_weight, np.float32(0), ((0, 127, 0),)) + lax.pad(
        band.astype(F32), np.float32(0), ((1, 126, 0),)
    )
    blocks = pl.pallas_call(
        packing,
        out_shape=jax.ShapeDtypeStruct((visits, rows, 128), F32),
        in_specs=[vmem] * 5,
        out_specs=vmem,
        compiler_params=params,
        name="pack",
    )(*loaded, meta[None])
    gathered = lax.all_to_all(blocks, "visit", 0, 0, tiled=True)
    edge = jax.ShapeDtypeStruct((bands, EDGE, 128), F32)
    near, first, second = pl.pallas_call(
        widen_kernel,
        out_shape=(jax.ShapeDtypeStruct((bands, rows, 128), F32), edge, edge),
        in_specs=[vmem] * 3,
        out_specs=[vmem] * 3,
        compiler_params=params,
        name="widen",
    )(tile, core, other)
    halo_a = lax.ppermute(first, "quad", swaps(quads, 0))
    halo_b = lax.ppermute(second, "quad", swaps(quads, 1))
    tables = [
        stay(jnp.asarray(array)) for array in (row_weights(rows),) + column_weights(cols, 64)
    ]
    return pl.pallas_call(
        modelling,
        out_shape=jax.ShapeDtypeStruct((bands, rows, cols), F32),
        in_specs=[vmem] * 4 + [hbm] * 3,
        out_specs=vmem,
        scratch_shapes=[
            pltpu.VMEM((bands, ext, 128), F32),
            pltpu.VMEM((bands, rows, 128), F32),
        ]
        + [pltpu.VMEM(a.shape, a.dtype) for a in tables]
        + [pltpu.SemaphoreType.DMA((3,))],
        compiler_params=params,
        name="model",
    )(gathered, near, halo_a, halo_b, *tables)


def solution(mesh):
    placed = (
        P(None, "quad", "visit"),
        P("visit", "quad", None),
        P("visit", "quad", None),
        P("visit", None, None),
        P("visit"),
        P("visit"),
        P("visit", "quad", None),
    )
    return jax.shard_map(
        per_device, mesh=mesh, in_specs=placed, out_specs=P(None, "quad", "visit"), check_vma=False
    )
```

```python
import functools

import jax
import jax.numpy as jnp
import numpy as np
from jax import lax
from jax.experimental import pallas as pl
from jax.experimental.pallas import tpu as pltpu
from jax.sharding import PartitionSpec as P


RAD = 10
EDGE = 16
SIGMAS = (1.0, 2.5, 5.0)
DEGREES = (4, 3, 2)
GROUP = 4
F32 = jnp.float32
BF16 = jnp.bfloat16


def taps(sigma, power):
    offsets = np.arange(-RAD, RAD + 1).astype(np.float64)
    bell = np.exp(-offsets * offsets / (2.0 * sigma * sigma))
    return bell / bell.sum() * (offsets / sigma) ** power


def band_matrix(positions, outs):
    tables = []
    for sigma, degree in zip(SIGMAS, DEGREES):
        for power in range(degree + 1):
            filt = taps(sigma, power)
            offset = positions[None, :] - np.arange(outs)[:, None]
            inside = np.abs(offset) <= RAD
            tables.append(np.where(inside, filt[np.clip(offset + RAD, 0, 2 * RAD)], 0.0))
    return np.stack(tables).astype(np.float32)


def split(array):
    high = array.astype(BF16)
    low = (array.astype(F32) - high.astype(F32)).astype(BF16)
    return high, low


def np_split(array):
    high = array.astype(jnp.bfloat16)
    low = (array - high.astype(np.float32)).astype(jnp.bfloat16)
    return high, low


def row_weights(rows):
    positions = np.concatenate(
        [np.arange(rows), np.arange(EDGE) - EDGE, rows + np.arange(EDGE)]
    )
    table = band_matrix(positions, rows).reshape(-1, rows + 2 * EDGE)
    high, low = np_split(table)
    return np.concatenate([high, high, low], axis=1)


def column_weights(cols, lanes):
    far = 10 * cols + 1000
    positions = np.concatenate(
        [
            np.arange(cols),
            np.arange(RAD) - RAD,
            cols + np.arange(RAD),
            np.full(lanes - cols - 2 * RAD, far),
        ]
    )
    table = band_matrix(positions, cols)
    count = table.shape[0]
    wide = np.zeros((GROUP, lanes, count, GROUP, cols), np.float32)
    for v in range(GROUP):
        wide[v, :, :, v, :] = table.transpose(2, 0, 1)
    return np_split(wide.reshape(GROUP * lanes, count * GROUP * cols))


def lanes_of(shape):
    return lax.broadcasted_iota(jnp.int32, shape, 1)


def packed(tiles, cols):
    lane = lanes_of(tiles[0].shape)
    out = []
    for b in range(0, len(tiles), GROUP):
        tile = tiles[b]
        for k in range(1, min(GROUP, len(tiles) - b)):
            tile = jnp.where(lane < k * cols, tile, pltpu.roll(tiles[b + k], k * cols, 1))
        out.append(tile)
    return out


def load_kernel(count, *refs):
    sources, refs = refs[:count], refs[count:]
    (first_ref, second_ref, wide_ref), refs = refs[:3], refs[3:]
    targets, (t_ref, sems) = refs[: count - 1], refs[count - 1 :]
    copies = [
        pltpu.make_async_copy(a, b, sems.at[i])
        for i, (a, b) in enumerate(zip(sources, (t_ref, *targets)))
    ]
    for copy in copies:
        copy.start()
    for copy in copies:
        copy.wait()
    bands, rows, cols = t_ref.shape
    even = lax.axis_index("quad") % 2 == 0
    wide_ref[:, :, 0:cols] = t_ref[...]
    for k, tile in enumerate(packed([wide_ref[b] for b in range(bands)], cols)):
        last, leading = tile[rows - EDGE :], tile[:EDGE]
        first_ref[k] = jnp.where(even, last, leading)
        second_ref[k] = jnp.where(even, leading, last)


def pack_kernel(
    visits, cols, sci_ref, var_ref, coef_ref, foot_ref, meta_ref, mine_ref, away_ref, blocks
):
    rows = sci_ref.shape[1]
    short = rows // 2
    chips = visits // 2
    me = lax.axis_index("visit")
    chip, side = me // 2, me % 2
    at = chips * short
    weight = jnp.broadcast_to(meta_ref[:, 0:1], (rows, 128))
    coef = coef_ref[:, 0, :]
    terms, basis = coef.shape
    which = jnp.broadcast_to(meta_ref[:, 1:2], (1, 128))
    for ref in (mine_ref, away_ref):
        ref[at : at + terms, 0:basis] = coef
        ref[at + terms : at + terms + 1] = which
    tile_rows, tile_cols = foot_ref.shape[1], foot_ref.shape[2]
    foot = foot_ref[0].astype(F32)
    width = sci_ref.shape[2]
    height = rows // tile_rows
    span = width // tile_cols
    per = 128 // span
    tcol = lax.broadcasted_iota(jnp.int32, (tile_cols, 128), 0)
    tlane = lanes_of((tile_cols, 128)) // span
    parts = []
    for chunk in range(width // 128):
        pick = jnp.where(tcol == tlane + chunk * per, 1.0, 0.0).astype(F32)
        cover = jnp.dot(foot, pick, preferred_element_type=F32)
        cover = jnp.concatenate(
            [jnp.broadcast_to(cover[k : k + 1], (height, 128)) for k in range(tile_rows)], axis=0
        )
        inside = slice(chunk * 128, chunk * 128 + 128)
        scale = weight * cover / var_ref[0, :, inside]
        parts.append((scale * sci_ref[0, :, inside], scale))
    flat = lanes_of((short, 128))
    for d in range(visits):
        whole, within = (d * cols) // 128, (d * cols) % 128
        first, second = parts[whole]
        pieces = (first[:short], first[short:], second[:short], second[short:])
        block = pltpu.roll(pieces[0], (128 - within) % 128, 1)
        for k in range(1, 4):
            turned = pltpu.roll(pieces[k], (128 + 32 * k - within) % 128, 1)
            block = jnp.where(flat < 32 * k, block, turned)
        blocks[d] = block
    for m in range(chips):
        other = chip ^ m
        mine_ref[m * short : (m + 1) * short] = blocks[2 * other + side]
        away_ref[m * short : (m + 1) * short] = blocks[2 * other + 1 - side]


def edge_kernel(cols, wide_ref, a_ref, b_ref, own_ref, out_ref):
    bands, rows, _ = wide_ref.shape
    ext = rows + 2 * EDGE
    lane = lanes_of((ext, 128))
    upper = lax.axis_index("quad") % 2 == 0
    left = jnp.zeros((ext, 128), F32)
    right = jnp.zeros((ext, 128), F32)
    for b in range(bands):
        halo = [
            pltpu.roll(ref[b // GROUP], (128 - (b % GROUP) * cols) % 128, 1)
            for ref in (a_ref, b_ref)
        ]
        north = jnp.where(upper, halo[1], halo[0])
        south = jnp.where(upper, halo[0], halo[1])
        tile = jnp.concatenate([wide_ref[b], north, south], axis=0)
        own_ref[b] = tile
        at = RAD * b
        here = (lane >= at) & (lane < at + RAD)
        left = jnp.where(here, pltpu.roll(tile, at, 1), left)
        right = jnp.where(here, pltpu.roll(tile, (at - (cols - RAD)) % 128, 1), right)
    even = lax.axis_index("visit") % 2 == 0
    inner = jnp.where(even, right, left)
    outer = jnp.where(even, left, right)
    out_ref[...] = jnp.where(lane < 64, inner, pltpu.roll(outer, 64, 1))


def merge_kernel(rows, steps, mine_ref, got_ref, edge_ref, *out_refs):
    chips = len(out_refs) + 1
    short = rows // 2
    base = chips * short
    half = lanes_of((rows, 128)) < 64
    middle = edge_ref.shape[0] // 2
    edge = jnp.where(
        half[:middle], pltpu.roll(edge_ref[:middle], 64, 1), edge_ref[middle:]
    )
    coefs = jnp.where(
        half[:8], mine_ref[base : base + 8], pltpu.roll(got_ref[base : base + 8], 64, 1)
    )
    for m in range(1, chips):
        out_ref = out_refs[m - 1]
        at = slice(m * short, (m + 1) * short)
        out_ref[0:short] = mine_ref[at]
        out_ref[short:rows] = got_ref[at]
        out_ref[rows : rows + 8] = coefs
        if m in steps:
            out_ref[rows + 8 : rows + 8 + middle] = edge


def table_kernel(*refs):
    refs, sems = refs[1:-1], refs[-1]
    count = len(refs) // 2
    copies = [
        pltpu.make_async_copy(refs[i], refs[count + i], sems.at[i]) for i in range(count)
    ]
    for copy in copies:
        copy.start()
    for copy in copies:
        copy.wait()


def choose(which, tiles):
    shape = tiles[0].shape
    which = jnp.broadcast_to(which, shape)
    picked = jnp.zeros(shape, F32)
    for b, tile in enumerate(tiles):
        picked = jnp.where(which == float(b), tile, picked)
    return picked


def model_kernel(
    visits, quads, steps, mine_ref, got_ref, own_ref, inner_ref, tab_ref, dh_ref, dl_ref, *refs
):
    message_refs, (out_ref, near) = refs[:-2], refs[-2:]
    bands, rows, cols = out_ref.shape
    short = rows // 2
    ext = rows + 2 * EDGE
    chips = visits // 2
    groups = visits // GROUP
    me = lax.axis_index("visit")
    quad = lax.axis_index("quad")
    chip = me // 2
    even = me % 2 == 0

    wide_lane = lanes_of((ext, 128))
    middle = ext // 2
    beside = jnp.where(even, chip - 1, chip + 1)
    exists = (beside >= 0) & (beside < chips)
    edge = jnp.zeros((middle, 128), F32)
    for m in steps:
        arrived = message_refs[m - 1][rows + 8 : rows + 8 + middle]
        edge = jnp.where(exists & ((chip ^ beside) == m), arrived, edge)
    outer = jnp.concatenate([edge, pltpu.roll(edge, 64, 1)], axis=0)
    inner = inner_ref[...]
    west = jnp.where(even, outer, inner)
    east = jnp.where(even, inner, outer)
    for b in range(bands):
        at = RAD * b
        tile = jnp.where(
            wide_lane < cols,
            own_ref[b],
            jnp.where(
                wide_lane < cols + RAD,
                pltpu.roll(west, (cols - at) % 128, 1),
                jnp.where(
                    wide_lane < cols + 2 * RAD,
                    pltpu.roll(east, (cols + RAD - at) % 128, 1),
                    0.0,
                ),
            ),
        )
        near[b] = jnp.where(wide_lane < 64, tile, pltpu.roll(tile, 64, 1))

    lane = lanes_of((rows, 128))
    flat = lane[:short]
    low_half = lane[:1] < 64
    x = (((lane % cols) + me * cols).astype(F32) + 0.5) / (visits * cols) * 2.0 - 1.0
    trow = lax.broadcasted_iota(jnp.int32, (rows, 256), 0)
    y = ((trow + quad * rows).astype(F32) + 0.5) / (quads * rows) * 2.0 - 1.0
    yy = y * y
    base = 8 * (lane // cols)
    base_row = chips * short
    slots = [
        (mine_ref, 0, mine_ref, base_row, False),
        (got_ref, 0, got_ref, base_row, False),
    ]
    for ref in message_refs:
        slots += [(ref, 0, ref, rows, False), (ref, short, ref, rows, True)]

    def gather(members):
        blocks, tails, band_rows = [], [], []
        for ref, at, tail_ref, tail_at, high in members:
            blocks.append(ref[at : at + short])
            tail = tail_ref[tail_at : tail_at + 8]
            turned = pltpu.roll(tail, 64, 1)
            tails.append(turned if high else tail)
            band_rows.append(jnp.where(low_half == (not high), tail[6:7], turned[6:7]))
        pieces = [jnp.zeros((short, 128), F32)] * 4
        which = jnp.zeros((1, 128), F32)
        for v in range(GROUP):
            here = (flat >= v * cols) & (flat < (v + 1) * cols)
            pieces = [
                jnp.where(here, pltpu.roll(blocks[v], (v * cols - 32 * k) % 128, 1), piece)
                for k, piece in enumerate(pieces)
            ]
            which = jnp.where(here[:1], band_rows[v], which)
        tails.append(jnp.zeros((128 - 8 * GROUP, 128), F32))
        cmat = jnp.transpose(jnp.concatenate(tails, axis=0))[0:rows]
        terms = [jnp.take_along_axis(cmat, base + s, axis=1) for s in range(6)]
        polys = (
            terms[0] + x * (terms[1] + x * terms[3]),
            terms[2] + x * terms[4],
            terms[5],
        )
        images = [
            choose(
                jnp.where(low_half, band_rows[2 * p], band_rows[2 * p + 1]),
                [near[b] for b in range(bands)],
            )
            for p in range(GROUP // 2)
        ]
        first = jnp.concatenate(pieces[:2], axis=0)
        second = jnp.concatenate(pieces[2:], axis=0)
        return polys, jnp.concatenate(images, axis=1), first, second, which

    totals = [jnp.zeros((rows, 128), F32) for _ in range(bands)]
    for start in range(0, groups, 2):
        pair = [gather(slots[g * GROUP : (g + 1) * GROUP]) for g in (start, start + 1)]
        parts = [split(image) for _, image, _, _, _ in pair]
        both = jnp.concatenate([p[0] for p in parts] + [p[1] for p in parts], axis=0)
        poly0, poly1, poly2 = [
            jnp.concatenate([pair[0][0][k], pair[1][0][k]], axis=1) for k in range(3)
        ]
        model = jnp.zeros((rows, 256), F32)
        basis_start = 0
        filt = 0
        for degree in DEGREES:
            count = degree + 1
            index = {}
            k = basis_start
            for i in range(count):
                for j in range(count - i):
                    index[i, j] = k
                    k += 1
            for j0 in range(0, count, 2):
                js = range(j0, min(j0 + 2, count))
                lanes = slice((filt + j0) * 128, (filt + js[-1] + 1) * 128)
                wide = jnp.dot(both, dh_ref[:, lanes], preferred_element_type=F32)
                conv = (
                    wide[: 2 * ext]
                    + wide[2 * ext :]
                    + jnp.dot(both[: 2 * ext], dl_ref[:, lanes], preferred_element_type=F32)
                )
                for j in js:
                    part = conv[:, (j - j0) * 128 : (j - j0 + 1) * 128]
                    part = jnp.concatenate([part[:ext], part[ext:]], axis=1)
                    high, low = split(part)
                    rowed = jnp.dot(
                        tab_ref[filt * rows : (filt + count - j) * rows],
                        jnp.concatenate([high, low, high], axis=0),
                        preferred_element_type=F32,
                    )
                    for i in range(count - j):
                        n = index[i, j]
                        spatial = (
                            poly0[n : n + 1] + y * poly1[n : n + 1] + yy * poly2[n : n + 1]
                        )
                        model = model + spatial * rowed[i * rows : (i + 1) * rows]
            basis_start = k
            filt += count
        for g in range(2):
            _, _, first, second, which = pair[g]
            part = first - second * model[:, g * 128 : (g + 1) * 128]
            which = jnp.broadcast_to(which, (rows, 128))
            for b in range(bands):
                totals[b] = totals[b] + jnp.where(which == float(b), part, 0.0)
    for b in range(bands):
        folded = totals[b] + pltpu.roll(totals[b], 64, 1)
        out_ref[b] = (folded + pltpu.roll(folded, 96, 1))[:, 0:cols]


def swaps(count, start):
    pairs = [(i, i + 1) for i in range(start, count - 1, 2)]
    return pairs + [(j, i) for i, j in pairs]


def stay(array):
    return pltpu.with_memory_space_constraint(array, pltpu.HBM)


def per_device(template, science, variance, coeffs, visit_weight, band, footprint):
    visits, quads = lax.axis_size("visit"), lax.axis_size("quad")
    chips = visits // 2
    bands, rows, cols = template.shape
    ext = rows + 2 * EDGE
    short = rows // 2
    vmem = pl.BlockSpec(memory_space=pltpu.VMEM)
    hbm = pl.BlockSpec(memory_space=pltpu.HBM)
    params = pltpu.CompilerParams(vmem_limit_bytes=24 * 1024 * 1024)
    struct = jax.ShapeDtypeStruct

    def call(kernel, outs, ins, scratch=()):
        return pl.pallas_call(
            kernel,
            out_shape=outs,
            in_specs=ins,
            out_specs=jax.tree.map(lambda _: vmem, outs),
            scratch_shapes=scratch,
            compiler_params=params,
        )

    turned = jnp.transpose(coeffs, (2, 0, 1))
    sources = [stay(array) for array in (template, science, variance, turned, footprint)]
    strip = struct((-(-bands // GROUP), EDGE, 128), F32)
    first, second, wide, *loaded = call(
        functools.partial(load_kernel, len(sources)),
        [strip, strip, struct((bands, rows, 128), F32)]
        + [struct(a.shape, a.dtype) for a in sources[1:]],
        [hbm] * 5,
        [pltpu.VMEM(template.shape, F32), pltpu.SemaphoreType.DMA((5,))],
    )(*sources)
    halo_a = lax.ppermute(first, "quad", swaps(quads, 0))
    halo_b = lax.ppermute(second, "quad", swaps(quads, 1))
    meta = lax.pad(visit_weight, np.float32(0), ((0, 127, 0),)) + lax.pad(
        band.astype(F32), np.float32(0), ((1, 126, 0),)
    )
    height = chips * short + 8
    mine, away = call(
        functools.partial(pack_kernel, visits, cols),
        [struct((height, 128), F32)] * 2,
        [vmem] * 5,
        [pltpu.VMEM((visits, short, 128), F32)],
    )(*loaded, meta[None])
    got = lax.ppermute(away, "visit", swaps(visits, 0))
    own, to_core = call(
        functools.partial(edge_kernel, cols),
        [struct((bands, ext, 128), F32), struct((ext, 128), F32)],
        [vmem] * 3,
    )(wide, halo_a, halo_b)
    edge = lax.ppermute(to_core, "visit", swaps(visits, 0))
    steps = sorted({c ^ (c + 1) for c in range(chips - 1)})
    outgoing = call(
        functools.partial(merge_kernel, rows, steps),
        [
            struct((rows + 8 + (ext // 2 if m in steps else 0), 128), F32)
            for m in range(1, chips)
        ],
        [vmem] * 3,
    )(mine, got, edge)
    incoming = [
        lax.ppermute(array, "visit", [(i, i ^ (2 * m)) for i in range(visits)])
        for m, array in enumerate(outgoing, 1)
    ]
    tables = [
        stay(jnp.asarray(array)) for array in (row_weights(rows),) + column_weights(cols, 64)
    ]
    tables = call(
        table_kernel,
        [struct(a.shape, a.dtype) for a in tables],
        [vmem] + [hbm] * 3,
        [pltpu.SemaphoreType.DMA((3,))],
    )(outgoing[0], *tables)
    return call(
        functools.partial(model_kernel, visits, quads, steps),
        struct((bands, rows, cols), F32),
        [vmem] * (7 + chips - 1),
        [pltpu.VMEM((bands, ext, 128), F32)],
    )(mine, got, own, edge, *tables, *incoming)


def solution(mesh):
    placed = (
        P(None, "quad", "visit"),
        P("visit", "quad", None),
        P("visit", "quad", None),
        P("visit", None, None),
        P("visit"),
        P("visit"),
        P("visit", "quad", None),
    )
    return jax.shard_map(
        per_device, mesh=mesh, in_specs=placed, out_specs=P(None, "quad", "visit"), check_vma=False
    )
```

```python
import functools

import jax
import jax.numpy as jnp
import numpy as np
from jax import lax
from jax.experimental import pallas as pl
from jax.experimental.pallas import tpu as pltpu
from jax.sharding import PartitionSpec as P


RAD = 10
EDGE = 16
SIGMAS = (1.0, 2.5, 5.0)
DEGREES = (4, 3, 2)
GROUP = 4
F32 = jnp.float32
BF16 = jnp.bfloat16


def taps(sigma, power):
    offsets = np.arange(-RAD, RAD + 1).astype(np.float64)
    bell = np.exp(-offsets * offsets / (2.0 * sigma * sigma))
    return bell / bell.sum() * (offsets / sigma) ** power


def band_matrix(positions, outs):
    tables = []
    for sigma, degree in zip(SIGMAS, DEGREES):
        for power in range(degree + 1):
            filt = taps(sigma, power)
            offset = positions[None, :] - np.arange(outs)[:, None]
            inside = np.abs(offset) <= RAD
            tables.append(np.where(inside, filt[np.clip(offset + RAD, 0, 2 * RAD)], 0.0))
    return np.stack(tables).astype(np.float32)


def split(array):
    high = array.astype(BF16)
    low = (array.astype(F32) - high.astype(F32)).astype(BF16)
    return high, low


def np_split(array):
    high = array.astype(jnp.bfloat16)
    low = (array - high.astype(np.float32)).astype(jnp.bfloat16)
    return high, low


def row_weights(rows):
    positions = np.concatenate(
        [np.arange(rows), np.arange(EDGE) - EDGE, rows + np.arange(EDGE)]
    )
    table = band_matrix(positions, rows).reshape(-1, rows + 2 * EDGE)
    high, low = np_split(table)
    return np.concatenate([high, high, low], axis=1)


def column_weights(cols, lanes):
    far = 10 * cols + 1000
    positions = np.concatenate(
        [
            np.arange(cols),
            np.arange(RAD) - RAD,
            cols + np.arange(RAD),
            np.full(lanes - cols - 2 * RAD, far),
        ]
    )
    table = band_matrix(positions, cols)
    count = table.shape[0]
    wide = np.zeros((GROUP, lanes, count, GROUP, cols), np.float32)
    for v in range(GROUP):
        wide[v, :, :, v, :] = table.transpose(2, 0, 1)
    return np_split(wide.reshape(GROUP * lanes, count * GROUP * cols))


def lanes_of(shape):
    return lax.broadcasted_iota(jnp.int32, shape, 1)


def packed(tiles, cols):
    lane = lanes_of(tiles[0].shape)
    out = []
    for b in range(0, len(tiles), GROUP):
        tile = tiles[b]
        for k in range(1, min(GROUP, len(tiles) - b)):
            tile = jnp.where(lane < k * cols, tile, pltpu.roll(tiles[b + k], k * cols, 1))
        out.append(tile)
    return out


def load_kernel(count, *refs):
    sources, refs = refs[:count], refs[count:]
    (first_ref, second_ref, wide_ref), refs = refs[:3], refs[3:]
    targets, (t_ref, sems) = refs[: count - 1], refs[count - 1 :]
    copies = [
        pltpu.make_async_copy(a, b, sems.at[i])
        for i, (a, b) in enumerate(zip(sources, (t_ref, *targets)))
    ]
    for copy in copies:
        copy.start()
    for copy in copies:
        copy.wait()
    bands, rows, cols = t_ref.shape
    wide_ref[:, :, 0:cols] = t_ref[...]
    for k, tile in enumerate(packed([wide_ref[b] for b in range(bands)], cols)):
        last, leading = tile[rows - EDGE :], tile[:EDGE]
        first_ref[k] = last
        second_ref[k] = leading


def pack_kernel(
    visits, cols, sci_ref, var_ref, coef_ref, foot_ref, meta_ref, mine_ref, away_ref, blocks
):
    rows = sci_ref.shape[1]
    short = rows // 2
    chips = visits // 2
    me = lax.axis_index("visit")
    chip, side = me // 2, me % 2
    at = chips * short
    weight = jnp.broadcast_to(meta_ref[:, 0:1], (rows, 128))
    coef = coef_ref[:, 0, :]
    terms, basis = coef.shape
    which = jnp.broadcast_to(meta_ref[:, 1:2], (1, 128))
    for ref in (mine_ref, away_ref):
        ref[at : at + terms, 0:basis] = coef
        ref[at + terms : at + terms + 1] = which
    tile_rows, tile_cols = foot_ref.shape[1], foot_ref.shape[2]
    foot = foot_ref[0].astype(F32)
    width = sci_ref.shape[2]
    height = rows // tile_rows
    span = width // tile_cols
    per = 128 // span
    tcol = lax.broadcasted_iota(jnp.int32, (tile_cols, 128), 0)
    tlane = lanes_of((tile_cols, 128)) // span
    parts = []
    for chunk in range(width // 128):
        pick = jnp.where(tcol == tlane + chunk * per, 1.0, 0.0).astype(F32)
        cover = jnp.dot(foot, pick, preferred_element_type=F32)
        cover = jnp.concatenate(
            [jnp.broadcast_to(cover[k : k + 1], (height, 128)) for k in range(tile_rows)], axis=0
        )
        inside = slice(chunk * 128, chunk * 128 + 128)
        scale = weight * cover / var_ref[0, :, inside]
        parts.append((scale * sci_ref[0, :, inside], scale))
    flat = lanes_of((short, 128))
    for d in range(visits):
        whole, within = (d * cols) // 128, (d * cols) % 128
        first, second = parts[whole]
        pieces = (first[:short], first[short:], second[:short], second[short:])
        block = pltpu.roll(pieces[0], (128 - within) % 128, 1)
        for k in range(1, 4):
            turned = pltpu.roll(pieces[k], (128 + 32 * k - within) % 128, 1)
            block = jnp.where(flat < 32 * k, block, turned)
        blocks[d] = block
    for m in range(chips):
        other = chip ^ m
        mine_ref[m * short : (m + 1) * short] = blocks[2 * other + side]
        away_ref[m * short : (m + 1) * short] = blocks[2 * other + 1 - side]


def edge_kernel(cols, quads, wide_ref, a_ref, b_ref, own_ref, out_ref):
    bands, rows, _ = wide_ref.shape
    ext = rows + 2 * EDGE
    lane = lanes_of((ext, 128))
    quad = lax.axis_index("quad")
    left = jnp.zeros((ext, 128), F32)
    right = jnp.zeros((ext, 128), F32)
    for b in range(bands):
        halo = [
            pltpu.roll(ref[b // GROUP], (128 - (b % GROUP) * cols) % 128, 1)
            for ref in (a_ref, b_ref)
        ]
        north = jnp.where(quad > 0, halo[0], 0.0)
        south = jnp.where(quad < quads - 1, halo[1], 0.0)
        tile = jnp.concatenate([wide_ref[b], north, south], axis=0)
        own_ref[b] = tile
        at = RAD * b
        here = (lane >= at) & (lane < at + RAD)
        left = jnp.where(here, pltpu.roll(tile, at, 1), left)
        right = jnp.where(here, pltpu.roll(tile, (at - (cols - RAD)) % 128, 1), right)
    even = lax.axis_index("visit") % 2 == 0
    inner = jnp.where(even, right, left)
    outer = jnp.where(even, left, right)
    out_ref[...] = jnp.where(lane < 64, inner, pltpu.roll(outer, 64, 1))


def merge_kernel(rows, steps, mine_ref, got_ref, edge_ref, *out_refs):
    chips = len(out_refs) + 1
    short = rows // 2
    base = chips * short
    half = lanes_of((rows, 128)) < 64
    middle = edge_ref.shape[0] // 2
    edge = jnp.where(
        half[:middle], pltpu.roll(edge_ref[:middle], 64, 1), edge_ref[middle:]
    )
    coefs = jnp.where(
        half[:8], mine_ref[base : base + 8], pltpu.roll(got_ref[base : base + 8], 64, 1)
    )
    for m in range(1, chips):
        out_ref = out_refs[m - 1]
        at = slice(m * short, (m + 1) * short)
        out_ref[0:short] = mine_ref[at]
        out_ref[short:rows] = got_ref[at]
        out_ref[rows : rows + 8] = coefs
        if m in steps:
            out_ref[rows + 8 : rows + 8 + middle] = edge


def table_kernel(*refs):
    refs, sems = refs[1:-1], refs[-1]
    count = len(refs) // 2
    copies = [
        pltpu.make_async_copy(refs[i], refs[count + i], sems.at[i]) for i in range(count)
    ]
    for copy in copies:
        copy.start()
    for copy in copies:
        copy.wait()


def choose(which, tiles):
    shape = tiles[0].shape
    which = jnp.broadcast_to(which, shape)
    picked = jnp.zeros(shape, F32)
    for b, tile in enumerate(tiles):
        picked = jnp.where(which == float(b), tile, picked)
    return picked


def model_kernel(
    visits, quads, steps, mine_ref, got_ref, own_ref, inner_ref, tab_ref, dh_ref, dl_ref, *refs
):
    message_refs, (out_ref, near, stack) = refs[:-3], refs[-3:]
    bands, rows, cols = out_ref.shape
    short = rows // 2
    ext = rows + 2 * EDGE
    chips = visits // 2
    groups = visits // GROUP
    me = lax.axis_index("visit")
    quad = lax.axis_index("quad")
    chip = me // 2
    even = me % 2 == 0

    wide_lane = lanes_of((ext, 128))
    middle = ext // 2
    beside = jnp.where(even, chip - 1, chip + 1)
    exists = (beside >= 0) & (beside < chips)
    edge = jnp.zeros((middle, 128), F32)
    for m in steps:
        arrived = message_refs[m - 1][rows + 8 : rows + 8 + middle]
        edge = jnp.where(exists & ((chip ^ beside) == m), arrived, edge)
    outer = jnp.concatenate([edge, pltpu.roll(edge, 64, 1)], axis=0)
    inner = inner_ref[...]
    west = jnp.where(even, outer, inner)
    east = jnp.where(even, inner, outer)
    for b in range(bands):
        at = RAD * b
        tile = jnp.where(
            wide_lane < cols,
            own_ref[b],
            jnp.where(
                wide_lane < cols + RAD,
                pltpu.roll(west, (cols - at) % 128, 1),
                jnp.where(
                    wide_lane < cols + 2 * RAD,
                    pltpu.roll(east, (cols + RAD - at) % 128, 1),
                    0.0,
                ),
            ),
        )
        near[b] = jnp.where(wide_lane < 64, tile, pltpu.roll(tile, 64, 1))

    lane = lanes_of((rows, 128))
    flat = lane[:short]
    low_half = lane[:1] < 64
    x = (((lane % cols) + me * cols).astype(F32) + 0.5) / (visits * cols) * 2.0 - 1.0
    trow = lax.broadcasted_iota(jnp.int32, (rows, 256), 0)
    y = ((trow + quad * rows).astype(F32) + 0.5) / (quads * rows) * 2.0 - 1.0
    yy = y * y
    base = 8 * (lane // cols)
    base_row = chips * short
    slots = [
        (mine_ref, 0, mine_ref, base_row, False),
        (got_ref, 0, got_ref, base_row, False),
    ]
    for ref in message_refs:
        slots += [(ref, 0, ref, rows, False), (ref, short, ref, rows, True)]

    def gather(members):
        blocks, tails, band_rows = [], [], []
        for ref, at, tail_ref, tail_at, high in members:
            blocks.append(ref[at : at + short])
            tail = tail_ref[tail_at : tail_at + 8]
            turned = pltpu.roll(tail, 64, 1)
            tails.append(turned if high else tail)
            band_rows.append(jnp.where(low_half == (not high), tail[6:7], turned[6:7]))
        pieces = [jnp.zeros((short, 128), F32)] * 4
        which = jnp.zeros((1, 128), F32)
        for v in range(GROUP):
            here = (flat >= v * cols) & (flat < (v + 1) * cols)
            pieces = [
                jnp.where(here, pltpu.roll(blocks[v], (v * cols - 32 * k) % 128, 1), piece)
                for k, piece in enumerate(pieces)
            ]
            which = jnp.where(here[:1], band_rows[v], which)
        tails.append(jnp.zeros((128 - 8 * GROUP, 128), F32))
        cmat = jnp.transpose(jnp.concatenate(tails, axis=0))[0:rows]
        terms = [jnp.take_along_axis(cmat, base + s, axis=1) for s in range(6)]
        polys = (
            terms[0] + x * (terms[1] + x * terms[3]),
            terms[2] + x * terms[4],
            terms[5],
        )
        images = [
            choose(
                jnp.where(low_half, band_rows[2 * p], band_rows[2 * p + 1]),
                [near[b] for b in range(bands)],
            )
            for p in range(GROUP // 2)
        ]
        first = jnp.concatenate(pieces[:2], axis=0)
        second = jnp.concatenate(pieces[2:], axis=0)
        return polys, jnp.concatenate(images, axis=1), first, second, which

    totals = [jnp.zeros((rows, 128), F32) for _ in range(bands)]
    for start in range(0, groups, 2):
        pair = [gather(slots[g * GROUP : (g + 1) * GROUP]) for g in (start, start + 1)]
        parts = [split(image) for _, image, _, _, _ in pair]
        both = jnp.concatenate([p[0] for p in parts] + [p[1] for p in parts], axis=0)
        poly0, poly1, poly2 = [
            jnp.concatenate([pair[0][0][k], pair[1][0][k]], axis=1) for k in range(3)
        ]
        filt = 0
        for degree in DEGREES:
            count = degree + 1
            for j0 in range(0, count, 2):
                js = range(j0, min(j0 + 2, count))
                lanes = slice((filt + j0) * 128, (filt + js[-1] + 1) * 128)
                wide = jnp.dot(both, dh_ref[:, lanes], preferred_element_type=F32)
                conv = (
                    wide[: 2 * ext]
                    + wide[2 * ext :]
                    + jnp.dot(both[: 2 * ext], dl_ref[:, lanes], preferred_element_type=F32)
                )
                for j in js:
                    part = conv[:, (j - j0) * 128 : (j - j0 + 1) * 128]
                    high, low = split(jnp.concatenate([part[:ext], part[ext:]], axis=1))
                    at = (filt + j) * 3 * ext
                    stack[at : at + ext] = high
                    stack[at + ext : at + 2 * ext] = low
                    stack[at + 2 * ext : at + 3 * ext] = high
            filt += count
        model = jnp.zeros((rows, 256), F32)
        basis_start = 0
        filt = 0
        for degree in DEGREES:
            count = degree + 1
            index = {}
            k = basis_start
            for i in range(count):
                for j in range(count - i):
                    index[i, j] = k
                    k += 1
            for j in range(count):
                at = (filt + j) * 3 * ext
                rowed = jnp.dot(
                    tab_ref[filt * rows : (filt + count - j) * rows],
                    stack[at : at + 3 * ext],
                    preferred_element_type=F32,
                )
                for i in range(count - j):
                    n = index[i, j]
                    spatial = poly0[n : n + 1] + y * poly1[n : n + 1] + yy * poly2[n : n + 1]
                    model = model + spatial * rowed[i * rows : (i + 1) * rows]
            basis_start = k
            filt += count
        for g in range(2):
            _, _, first, second, which = pair[g]
            part = first - second * model[:, g * 128 : (g + 1) * 128]
            which = jnp.broadcast_to(which, (rows, 128))
            for b in range(bands):
                totals[b] = totals[b] + jnp.where(which == float(b), part, 0.0)
    for b in range(bands):
        folded = totals[b] + pltpu.roll(totals[b], 64, 1)
        out_ref[b] = (folded + pltpu.roll(folded, 96, 1))[:, 0:cols]


def swaps(count, start):
    pairs = [(i, i + 1) for i in range(start, count - 1, 2)]
    return pairs + [(j, i) for i, j in pairs]


def stay(array):
    return pltpu.with_memory_space_constraint(array, pltpu.HBM)


def per_device(template, science, variance, coeffs, visit_weight, band, footprint):
    visits, quads = lax.axis_size("visit"), lax.axis_size("quad")
    chips = visits // 2
    bands, rows, cols = template.shape
    ext = rows + 2 * EDGE
    short = rows // 2
    vmem = pl.BlockSpec(memory_space=pltpu.VMEM)
    hbm = pl.BlockSpec(memory_space=pltpu.HBM)
    params = pltpu.CompilerParams(vmem_limit_bytes=24 * 1024 * 1024)
    struct = jax.ShapeDtypeStruct

    def call(kernel, outs, ins, scratch=()):
        return pl.pallas_call(
            kernel,
            out_shape=outs,
            in_specs=ins,
            out_specs=jax.tree.map(lambda _: vmem, outs),
            scratch_shapes=scratch,
            compiler_params=params,
        )

    turned = jnp.transpose(coeffs, (2, 0, 1))
    sources = [stay(array) for array in (template, science, variance, turned, footprint)]
    strip = struct((-(-bands // GROUP), EDGE, 128), F32)
    first, second, wide, *loaded = call(
        functools.partial(load_kernel, len(sources)),
        [strip, strip, struct((bands, rows, 128), F32)]
        + [struct(a.shape, a.dtype) for a in sources[1:]],
        [hbm] * 5,
        [pltpu.VMEM(template.shape, F32), pltpu.SemaphoreType.DMA((5,))],
    )(*sources)
    halo_a = lax.ppermute(first, "quad", [(i, (i + 1) % quads) for i in range(quads)])
    halo_b = lax.ppermute(second, "quad", [((i + 1) % quads, i) for i in range(quads)])
    meta = lax.pad(visit_weight, np.float32(0), ((0, 127, 0),)) + lax.pad(
        band.astype(F32), np.float32(0), ((1, 126, 0),)
    )
    height = chips * short + 8
    mine, away = call(
        functools.partial(pack_kernel, visits, cols),
        [struct((height, 128), F32)] * 2,
        [vmem] * 5,
        [pltpu.VMEM((visits, short, 128), F32)],
    )(*loaded, meta[None])
    got = lax.ppermute(away, "visit", swaps(visits, 0))
    own, to_core = call(
        functools.partial(edge_kernel, cols, quads),
        [struct((bands, ext, 128), F32), struct((ext, 128), F32)],
        [vmem] * 3,
    )(wide, halo_a, halo_b)
    edge = lax.ppermute(to_core, "visit", swaps(visits, 0))
    steps = sorted({c ^ (c + 1) for c in range(chips - 1)})
    outgoing = call(
        functools.partial(merge_kernel, rows, steps),
        [
            struct((rows + 8 + (ext // 2 if m in steps else 0), 128), F32)
            for m in range(1, chips)
        ],
        [vmem] * 3,
    )(mine, got, edge)
    incoming = [
        lax.ppermute(array, "visit", [(i, i ^ (2 * m)) for i in range(visits)])
        for m, array in enumerate(outgoing, 1)
    ]
    tables = [
        stay(jnp.asarray(array)) for array in (row_weights(rows),) + column_weights(cols, 64)
    ]
    tables = call(
        table_kernel,
        [struct(a.shape, a.dtype) for a in tables],
        [vmem] + [hbm] * 3,
        [pltpu.SemaphoreType.DMA((3,))],
    )(outgoing[0], *tables)
    return call(
        functools.partial(model_kernel, visits, quads, steps),
        struct((bands, rows, cols), F32),
        [vmem] * (7 + chips - 1),
        [pltpu.VMEM((bands, ext, 128), F32), pltpu.VMEM((12 * 3 * ext, 256), BF16)],
    )(mine, got, own, edge, *tables, *incoming)


def solution(mesh):
    placed = (
        P(None, "quad", "visit"),
        P("visit", "quad", None),
        P("visit", "quad", None),
        P("visit", None, None),
        P("visit"),
        P("visit"),
        P("visit", "quad", None),
    )
    return jax.shard_map(
        per_device, mesh=mesh, in_specs=placed, out_specs=P(None, "quad", "visit"), check_vma=False
    )
```

```python
import functools

import jax
import jax.numpy as jnp
import numpy as np
from jax import lax
from jax.experimental import pallas as pl
from jax.experimental.pallas import tpu as pltpu
from jax.sharding import PartitionSpec as P


RAD = 10
EDGE = 16
SIGMAS = (1.0, 2.5, 5.0)
DEGREES = (4, 3, 2)
GROUP = 4
F32 = jnp.float32
BF16 = jnp.bfloat16


def taps(sigma, power):
    offsets = np.arange(-RAD, RAD + 1).astype(np.float64)
    bell = np.exp(-offsets * offsets / (2.0 * sigma * sigma))
    return bell / bell.sum() * (offsets / sigma) ** power


def band_matrix(positions, outs):
    tables = []
    for sigma, degree in zip(SIGMAS, DEGREES):
        for power in range(degree + 1):
            filt = taps(sigma, power)
            offset = positions[None, :] - np.arange(outs)[:, None]
            inside = np.abs(offset) <= RAD
            tables.append(np.where(inside, filt[np.clip(offset + RAD, 0, 2 * RAD)], 0.0))
    return np.stack(tables).astype(np.float32)


def split(array):
    high = array.astype(BF16)
    low = (array.astype(F32) - high.astype(F32)).astype(BF16)
    return high, low


def np_split(array):
    high = array.astype(jnp.bfloat16)
    low = (array - high.astype(np.float32)).astype(jnp.bfloat16)
    return high, low


def row_weights(rows):
    positions = np.concatenate(
        [np.arange(rows), np.arange(EDGE) - EDGE, rows + np.arange(EDGE)]
    )
    table = band_matrix(positions, rows).reshape(-1, rows + 2 * EDGE)
    high, low = np_split(table)
    return np.concatenate([high, high, low], axis=1)


def column_weights(cols, lanes):
    far = 10 * cols + 1000
    positions = np.concatenate(
        [
            np.arange(cols),
            np.arange(RAD) - RAD,
            cols + np.arange(RAD),
            np.full(lanes - cols - 2 * RAD, far),
        ]
    )
    table = band_matrix(positions, cols)
    count = table.shape[0]
    wide = np.zeros((GROUP, lanes, count, GROUP, cols), np.float32)
    for v in range(GROUP):
        wide[v, :, :, v, :] = table.transpose(2, 0, 1)
    return np_split(wide.reshape(GROUP * lanes, count * GROUP * cols))


def lanes_of(shape):
    return lax.broadcasted_iota(jnp.int32, shape, 1)


def packed(tiles, cols):
    lane = lanes_of(tiles[0].shape)
    out = []
    for b in range(0, len(tiles), GROUP):
        tile = tiles[b]
        for k in range(1, min(GROUP, len(tiles) - b)):
            tile = jnp.where(lane < k * cols, tile, pltpu.roll(tiles[b + k], k * cols, 1))
        out.append(tile)
    return out


def load_kernel(count, *refs):
    sources, refs = refs[:count], refs[count:]
    (first_ref, second_ref, wide_ref), refs = refs[:3], refs[3:]
    targets, (t_ref, sems) = refs[: count - 1], refs[count - 1 :]
    copies = [
        pltpu.make_async_copy(a, b, sems.at[i])
        for i, (a, b) in enumerate(zip(sources, (t_ref, *targets)))
    ]
    for copy in copies:
        copy.start()
    for copy in copies:
        copy.wait()
    bands, rows, cols = t_ref.shape
    wide_ref[:, :, 0:cols] = t_ref[...]
    for k, tile in enumerate(packed([wide_ref[b] for b in range(bands)], cols)):
        last, leading = tile[rows - EDGE :], tile[:EDGE]
        first_ref[k] = last
        second_ref[k] = leading


def pack_kernel(
    visits, cols, sci_ref, var_ref, coef_ref, foot_ref, meta_ref, mine_ref, away_ref, blocks
):
    rows = sci_ref.shape[1]
    short = rows // 2
    chips = visits // 2
    me = lax.axis_index("visit")
    chip, side = me // 2, me % 2
    at = chips * short
    weight = jnp.broadcast_to(meta_ref[:, 0:1], (rows, 128))
    coef = coef_ref[:, 0, :]
    terms, basis = coef.shape
    which = jnp.broadcast_to(meta_ref[:, 1:2], (1, 128))
    for ref in (mine_ref, away_ref):
        ref[at : at + terms, 0:basis] = coef
        ref[at + terms : at + terms + 1] = which
    tile_rows, tile_cols = foot_ref.shape[1], foot_ref.shape[2]
    foot = foot_ref[0].astype(F32)
    width = sci_ref.shape[2]
    height = rows // tile_rows
    span = width // tile_cols
    per = 128 // span
    tcol = lax.broadcasted_iota(jnp.int32, (tile_cols, 128), 0)
    tlane = lanes_of((tile_cols, 128)) // span
    parts = []
    for chunk in range(width // 128):
        pick = jnp.where(tcol == tlane + chunk * per, 1.0, 0.0).astype(F32)
        cover = jnp.dot(foot, pick, preferred_element_type=F32)
        cover = jnp.concatenate(
            [jnp.broadcast_to(cover[k : k + 1], (height, 128)) for k in range(tile_rows)], axis=0
        )
        inside = slice(chunk * 128, chunk * 128 + 128)
        scale = weight * cover / var_ref[0, :, inside]
        parts.append((scale * sci_ref[0, :, inside], scale))
    flat = lanes_of((short, 128))
    for d in range(visits):
        whole, within = (d * cols) // 128, (d * cols) % 128
        first, second = parts[whole]
        pieces = (first[:short], first[short:], second[:short], second[short:])
        block = pltpu.roll(pieces[0], (128 - within) % 128, 1)
        for k in range(1, 4):
            turned = pltpu.roll(pieces[k], (128 + 32 * k - within) % 128, 1)
            block = jnp.where(flat < 32 * k, block, turned)
        blocks[d] = block
    for m in range(chips):
        near = side if m == 0 else 1 - side
        other = chip ^ m
        mine_ref[m * short : (m + 1) * short] = blocks[2 * other + near]
        away_ref[m * short : (m + 1) * short] = blocks[2 * other + 1 - near]


def edge_kernel(cols, quads, wide_ref, a_ref, b_ref, own_ref, inner_ref, outer_ref):
    bands, rows, _ = wide_ref.shape
    ext = rows + 2 * EDGE
    lane = lanes_of((ext, 128))
    quad = lax.axis_index("quad")
    left = jnp.zeros((ext, 128), F32)
    right = jnp.zeros((ext, 128), F32)
    for b in range(bands):
        halo = [
            pltpu.roll(ref[b // GROUP], (128 - (b % GROUP) * cols) % 128, 1)
            for ref in (a_ref, b_ref)
        ]
        north = jnp.where(quad > 0, halo[0], 0.0)
        south = jnp.where(quad < quads - 1, halo[1], 0.0)
        tile = jnp.concatenate([wide_ref[b], north, south], axis=0)
        own_ref[b] = tile
        at = RAD * b
        here = (lane >= at) & (lane < at + RAD)
        left = jnp.where(here, pltpu.roll(tile, at, 1), left)
        right = jnp.where(here, pltpu.roll(tile, (at - (cols - RAD)) % 128, 1), right)
    even = lax.axis_index("visit") % 2 == 0
    half = lane[: ext // 2] < 64
    for ref, edge in (
        (inner_ref, jnp.where(even, right, left)),
        (outer_ref, jnp.where(even, left, right)),
    ):
        ref[...] = jnp.where(half, edge[: ext // 2], pltpu.roll(edge[ext // 2 :], 64, 1))


def merge_kernel(rows, steps, mine_ref, got_ref, edge_ref, *out_refs):
    chips = len(out_refs) + 1
    short = rows // 2
    base = chips * short
    middle = edge_ref.shape[0]
    coefs = jnp.where(
        lanes_of((8, 128)) < 64,
        mine_ref[base : base + 8],
        pltpu.roll(got_ref[base : base + 8], 64, 1),
    )
    for m in range(1, chips):
        out_ref = out_refs[m - 1]
        at = slice(m * short, (m + 1) * short)
        out_ref[0:short] = mine_ref[at]
        out_ref[short:rows] = got_ref[at]
        out_ref[rows : rows + 8] = coefs
        if m in steps:
            out_ref[rows + 8 : rows + 8 + middle] = edge_ref[...]


def table_kernel(*refs):
    refs, sems = refs[1:-1], refs[-1]
    count = len(refs) // 2
    copies = [
        pltpu.make_async_copy(refs[i], refs[count + i], sems.at[i]) for i in range(count)
    ]
    for copy in copies:
        copy.start()
    for copy in copies:
        copy.wait()


def choose(which, tiles):
    shape = tiles[0].shape
    which = jnp.broadcast_to(which, shape)
    picked = jnp.zeros(shape, F32)
    for b, tile in enumerate(tiles):
        picked = jnp.where(which == float(b), tile, picked)
    return picked


def model_kernel(
    visits, quads, steps, mine_ref, got_ref, own_ref, inner_ref, tab_ref, dh_ref, dl_ref, *refs
):
    message_refs, (out_ref, near, stack) = refs[:-3], refs[-3:]
    bands, rows, cols = out_ref.shape
    short = rows // 2
    ext = rows + 2 * EDGE
    chips = visits // 2
    groups = visits // GROUP
    me = lax.axis_index("visit")
    quad = lax.axis_index("quad")
    chip = me // 2
    even = me % 2 == 0

    wide_lane = lanes_of((ext, 128))
    middle = ext // 2
    beside = jnp.where(even, chip - 1, chip + 1)
    exists = (beside >= 0) & (beside < chips)
    edge = jnp.zeros((middle, 128), F32)
    for m in steps:
        arrived = message_refs[m - 1][rows + 8 : rows + 8 + middle]
        edge = jnp.where(exists & ((chip ^ beside) == m), arrived, edge)
    outer, inner = [
        jnp.concatenate([part, pltpu.roll(part, 64, 1)], axis=0) for part in (edge, inner_ref[...])
    ]
    west = jnp.where(even, outer, inner)
    east = jnp.where(even, inner, outer)
    for b in range(bands):
        at = RAD * b
        tile = jnp.where(
            wide_lane < cols,
            own_ref[b],
            jnp.where(
                wide_lane < cols + RAD,
                pltpu.roll(west, (cols - at) % 128, 1),
                jnp.where(
                    wide_lane < cols + 2 * RAD,
                    pltpu.roll(east, (cols + RAD - at) % 128, 1),
                    0.0,
                ),
            ),
        )
        near[b] = jnp.where(wide_lane < 64, tile, pltpu.roll(tile, 64, 1))

    lane = lanes_of((rows, 128))
    flat = lane[:short]
    low_half = lane[:1] < 64
    x = (((lane % cols) + me * cols).astype(F32) + 0.5) / (visits * cols) * 2.0 - 1.0
    trow = lax.broadcasted_iota(jnp.int32, (rows, 256), 0)
    y = ((trow + quad * rows).astype(F32) + 0.5) / (quads * rows) * 2.0 - 1.0
    yy = y * y
    base = 8 * (lane // cols)
    base_row = chips * short
    slots = [
        (mine_ref, 0, mine_ref, base_row, False),
        (got_ref, 0, got_ref, base_row, False),
    ]
    for ref in message_refs:
        slots += [(ref, 0, ref, rows, False), (ref, short, ref, rows, True)]

    def gather(members):
        blocks, tails, band_rows = [], [], []
        for ref, at, tail_ref, tail_at, high in members:
            blocks.append(ref[at : at + short])
            tail = tail_ref[tail_at : tail_at + 8]
            turned = pltpu.roll(tail, 64, 1)
            tails.append(turned if high else tail)
            band_rows.append(jnp.where(low_half == (not high), tail[6:7], turned[6:7]))
        pieces = [jnp.zeros((short, 128), F32)] * 4
        which = jnp.zeros((1, 128), F32)
        for v in range(GROUP):
            here = (flat >= v * cols) & (flat < (v + 1) * cols)
            pieces = [
                jnp.where(here, pltpu.roll(blocks[v], (v * cols - 32 * k) % 128, 1), piece)
                for k, piece in enumerate(pieces)
            ]
            which = jnp.where(here[:1], band_rows[v], which)
        tails.append(jnp.zeros((128 - 8 * GROUP, 128), F32))
        cmat = jnp.transpose(jnp.concatenate(tails, axis=0))[0:rows]
        terms = [jnp.take_along_axis(cmat, base + s, axis=1) for s in range(6)]
        polys = (
            terms[0] + x * (terms[1] + x * terms[3]),
            terms[2] + x * terms[4],
            terms[5],
        )
        images = [
            choose(
                jnp.where(low_half, band_rows[2 * p], band_rows[2 * p + 1]),
                [near[b] for b in range(bands)],
            )
            for p in range(GROUP // 2)
        ]
        first = jnp.concatenate(pieces[:2], axis=0)
        second = jnp.concatenate(pieces[2:], axis=0)
        return polys, jnp.concatenate(images, axis=1), first, second, which

    totals = [jnp.zeros((rows, 128), F32) for _ in range(bands)]
    for start in range(0, groups, 2):
        pair = [gather(slots[g * GROUP : (g + 1) * GROUP]) for g in (start, start + 1)]
        parts = [split(image) for _, image, _, _, _ in pair]
        both = jnp.concatenate([p[0] for p in parts] + [p[1] for p in parts], axis=0)
        poly0, poly1, poly2 = [
            jnp.concatenate([pair[0][0][k], pair[1][0][k]], axis=1) for k in range(3)
        ]
        filt = 0
        for degree in DEGREES:
            count = degree + 1
            for j0 in range(0, count, 2):
                js = range(j0, min(j0 + 2, count))
                lanes = slice((filt + j0) * 128, (filt + js[-1] + 1) * 128)
                wide = jnp.dot(both, dh_ref[:, lanes], preferred_element_type=F32)
                conv = (
                    wide[: 2 * ext]
                    + wide[2 * ext :]
                    + jnp.dot(both[: 2 * ext], dl_ref[:, lanes], preferred_element_type=F32)
                )
                for j in js:
                    part = conv[:, (j - j0) * 128 : (j - j0 + 1) * 128]
                    high, low = split(jnp.concatenate([part[:ext], part[ext:]], axis=1))
                    at = (filt + j) * 3 * ext
                    stack[at : at + ext] = high
                    stack[at + ext : at + 2 * ext] = low
                    stack[at + 2 * ext : at + 3 * ext] = high
            filt += count
        model = jnp.zeros((rows, 256), F32)
        basis_start = 0
        filt = 0
        for degree in DEGREES:
            count = degree + 1
            index = {}
            k = basis_start
            for i in range(count):
                for j in range(count - i):
                    index[i, j] = k
                    k += 1
            for j in range(count):
                at = (filt + j) * 3 * ext
                rowed = jnp.dot(
                    tab_ref[filt * rows : (filt + count - j) * rows],
                    stack[at : at + 3 * ext],
                    preferred_element_type=F32,
                )
                for i in range(count - j):
                    n = index[i, j]
                    spatial = poly0[n : n + 1] + y * poly1[n : n + 1] + yy * poly2[n : n + 1]
                    model = model + spatial * rowed[i * rows : (i + 1) * rows]
            basis_start = k
            filt += count
        for g in range(2):
            _, _, first, second, which = pair[g]
            part = first - second * model[:, g * 128 : (g + 1) * 128]
            which = jnp.broadcast_to(which, (rows, 128))
            for b in range(bands):
                totals[b] = totals[b] + jnp.where(which == float(b), part, 0.0)
    for b in range(bands):
        folded = totals[b] + pltpu.roll(totals[b], 64, 1)
        out_ref[b] = (folded + pltpu.roll(folded, 96, 1))[:, 0:cols]


def swaps(count, start):
    pairs = [(i, i + 1) for i in range(start, count - 1, 2)]
    return pairs + [(j, i) for i, j in pairs]


def stay(array):
    return pltpu.with_memory_space_constraint(array, pltpu.HBM)


def per_device(template, science, variance, coeffs, visit_weight, band, footprint):
    visits, quads = lax.axis_size("visit"), lax.axis_size("quad")
    chips = visits // 2
    bands, rows, cols = template.shape
    ext = rows + 2 * EDGE
    short = rows // 2
    vmem = pl.BlockSpec(memory_space=pltpu.VMEM)
    hbm = pl.BlockSpec(memory_space=pltpu.HBM)
    params = pltpu.CompilerParams(vmem_limit_bytes=24 * 1024 * 1024)
    struct = jax.ShapeDtypeStruct

    def call(kernel, outs, ins, scratch=()):
        return pl.pallas_call(
            kernel,
            out_shape=outs,
            in_specs=ins,
            out_specs=jax.tree.map(lambda _: vmem, outs),
            scratch_shapes=scratch,
            compiler_params=params,
        )

    turned = jnp.transpose(coeffs, (2, 0, 1))
    sources = [stay(array) for array in (template, science, variance, turned, footprint)]
    strip = struct((-(-bands // GROUP), EDGE, 128), F32)
    first, second, wide, *loaded = call(
        functools.partial(load_kernel, len(sources)),
        [strip, strip, struct((bands, rows, 128), F32)]
        + [struct(a.shape, a.dtype) for a in sources[1:]],
        [hbm] * 5,
        [pltpu.VMEM(template.shape, F32), pltpu.SemaphoreType.DMA((5,))],
    )(*sources)
    halo_a = lax.ppermute(first, "quad", [(i, (i + 1) % quads) for i in range(quads)])
    halo_b = lax.ppermute(second, "quad", [((i + 1) % quads, i) for i in range(quads)])
    meta = lax.pad(visit_weight, np.float32(0), ((0, 127, 0),)) + lax.pad(
        band.astype(F32), np.float32(0), ((1, 126, 0),)
    )
    height = chips * short + 8
    mine, away = call(
        functools.partial(pack_kernel, visits, cols),
        [struct((height, 128), F32)] * 2,
        [vmem] * 5,
        [pltpu.VMEM((visits, short, 128), F32)],
    )(*loaded, meta[None])
    got = lax.ppermute(away, "visit", swaps(visits, 0))
    own, to_core, to_chips = call(
        functools.partial(edge_kernel, cols, quads),
        [struct((bands, ext, 128), F32)] + [struct((ext // 2, 128), F32)] * 2,
        [vmem] * 3,
    )(wide, halo_a, halo_b)
    edge = lax.ppermute(to_core, "visit", swaps(visits, 0))
    steps = sorted({c ^ (c + 1) for c in range(chips - 1)})
    outgoing = call(
        functools.partial(merge_kernel, rows, steps),
        [
            struct((rows + 8 + (ext // 2 if m in steps else 0), 128), F32)
            for m in range(1, chips)
        ],
        [vmem] * 3,
    )(mine, got, to_chips)
    incoming = [
        lax.ppermute(array, "visit", [(i, i ^ (2 * m + 1)) for i in range(visits)])
        for m, array in enumerate(outgoing, 1)
    ]
    tables = [
        stay(jnp.asarray(array)) for array in (row_weights(rows),) + column_weights(cols, 64)
    ]
    tables = call(
        table_kernel,
        [struct(a.shape, a.dtype) for a in tables],
        [vmem] + [hbm] * 3,
        [pltpu.SemaphoreType.DMA((3,))],
    )(outgoing[0], *tables)
    return call(
        functools.partial(model_kernel, visits, quads, steps),
        struct((bands, rows, cols), F32),
        [vmem] * (7 + chips - 1),
        [pltpu.VMEM((bands, ext, 128), F32), pltpu.VMEM((12 * 3 * ext, 256), BF16)],
    )(mine, got, own, edge, *tables, *incoming)


def solution(mesh):
    placed = (
        P(None, "quad", "visit"),
        P("visit", "quad", None),
        P("visit", "quad", None),
        P("visit", None, None),
        P("visit"),
        P("visit"),
        P("visit", "quad", None),
    )
    return jax.shard_map(
        per_device, mesh=mesh, in_specs=placed, out_specs=P(None, "quad", "visit"), check_vma=False
    )
```

```python
import functools

import jax
import jax.numpy as jnp
import numpy as np
from jax import lax
from jax.experimental import pallas as pl
from jax.experimental.pallas import tpu as pltpu
from jax.sharding import PartitionSpec as P


RAD = 10
EDGE = 16
SIGMAS = (1.0, 2.5, 5.0)
DEGREES = (4, 3, 2)
GROUP = 4
F32 = jnp.float32
BF16 = jnp.bfloat16


def taps(sigma, power):
    offsets = np.arange(-RAD, RAD + 1).astype(np.float64)
    bell = np.exp(-offsets * offsets / (2.0 * sigma * sigma))
    return bell / bell.sum() * (offsets / sigma) ** power


def band_matrix(positions, outs):
    tables = []
    for sigma, degree in zip(SIGMAS, DEGREES):
        for power in range(degree + 1):
            filt = taps(sigma, power)
            offset = positions[None, :] - np.arange(outs)[:, None]
            inside = np.abs(offset) <= RAD
            tables.append(np.where(inside, filt[np.clip(offset + RAD, 0, 2 * RAD)], 0.0))
    return np.stack(tables).astype(np.float32)


def split(array):
    high = array.astype(BF16)
    low = (array.astype(F32) - high.astype(F32)).astype(BF16)
    return high, low


def np_split(array):
    high = array.astype(jnp.bfloat16)
    low = (array - high.astype(np.float32)).astype(jnp.bfloat16)
    return high, low


def row_weights(rows):
    positions = np.concatenate(
        [np.arange(rows), np.arange(EDGE) - EDGE, rows + np.arange(EDGE)]
    )
    table = band_matrix(positions, rows).reshape(-1, rows + 2 * EDGE)
    high, low = np_split(table)
    return np.concatenate([high, high, low], axis=1)


def column_weights(cols, lanes):
    far = 10 * cols + 1000
    positions = np.concatenate(
        [
            np.arange(cols),
            np.arange(RAD) - RAD,
            cols + np.arange(RAD),
            np.full(lanes - cols - 2 * RAD, far),
        ]
    )
    table = band_matrix(positions, cols)
    count = table.shape[0]
    wide = np.zeros((GROUP, lanes, count, GROUP, cols), np.float32)
    for v in range(GROUP):
        wide[v, :, :, v, :] = table.transpose(2, 0, 1)
    return np_split(wide.reshape(GROUP * lanes, count * GROUP * cols))


def lanes_of(shape):
    return lax.broadcasted_iota(jnp.int32, shape, 1)


def packed(tiles, cols):
    lane = lanes_of(tiles[0].shape)
    out = []
    for b in range(0, len(tiles), GROUP):
        tile = tiles[b]
        for k in range(1, min(GROUP, len(tiles) - b)):
            tile = jnp.where(lane < k * cols, tile, pltpu.roll(tiles[b + k], k * cols, 1))
        out.append(tile)
    return out


def load_kernel(count, *refs):
    sources, refs = refs[:count], refs[count:]
    (first_ref, second_ref, wide_ref), refs = refs[:3], refs[3:]
    targets, (t_ref, sems) = refs[: count - 1], refs[count - 1 :]
    copies = [
        pltpu.make_async_copy(a, b, sems.at[i])
        for i, (a, b) in enumerate(zip(sources, (t_ref, *targets)))
    ]
    for copy in copies:
        copy.start()
    for copy in copies:
        copy.wait()
    bands, rows, cols = t_ref.shape
    wide_ref[:, :, 0:cols] = t_ref[...]
    for k, tile in enumerate(packed([wide_ref[b] for b in range(bands)], cols)):
        last, leading = tile[rows - EDGE :], tile[:EDGE]
        first_ref[k] = last
        second_ref[k] = leading


def pack_kernel(
    visits, cols, sci_ref, var_ref, coef_ref, foot_ref, w_ref, band_ref, mine_ref, away_ref, blocks
):
    rows = sci_ref.shape[1]
    short = rows // 2
    chips = visits // 2
    me = lax.axis_index("visit")
    chip, side = me // 2, me % 2
    at = chips * short
    weight = w_ref[0]
    coef = coef_ref[:, 0, :]
    terms, basis = coef.shape
    which = jnp.full((1, 128), band_ref[0].astype(F32), F32)
    for ref in (mine_ref, away_ref):
        ref[at : at + terms, 0:basis] = coef
        ref[at + terms : at + terms + 1] = which
    tile_rows, tile_cols = foot_ref.shape[1], foot_ref.shape[2]
    foot = foot_ref[0].astype(F32)
    width = sci_ref.shape[2]
    height = rows // tile_rows
    span = width // tile_cols
    per = 128 // span
    tcol = lax.broadcasted_iota(jnp.int32, (tile_cols, 128), 0)
    tlane = lanes_of((tile_cols, 128)) // span
    parts = []
    for chunk in range(width // 128):
        pick = jnp.where(tcol == tlane + chunk * per, 1.0, 0.0).astype(F32)
        cover = jnp.dot(foot, pick, preferred_element_type=F32)
        cover = jnp.concatenate(
            [jnp.broadcast_to(cover[k : k + 1], (height, 128)) for k in range(tile_rows)], axis=0
        )
        inside = slice(chunk * 128, chunk * 128 + 128)
        scale = weight * cover / var_ref[0, :, inside]
        parts.append((scale * sci_ref[0, :, inside], scale))
    flat = lanes_of((short, 128))
    for d in range(visits):
        whole, within = (d * cols) // 128, (d * cols) % 128
        first, second = parts[whole]
        pieces = (first[:short], first[short:], second[:short], second[short:])
        block = pltpu.roll(pieces[0], (128 - within) % 128, 1)
        for k in range(1, 4):
            turned = pltpu.roll(pieces[k], (128 + 32 * k - within) % 128, 1)
            block = jnp.where(flat < 32 * k, block, turned)
        blocks[d] = block
    for m in range(chips):
        near = side if m == 0 else 1 - side
        other = chip ^ m
        mine_ref[m * short : (m + 1) * short] = blocks[2 * other + near]
        away_ref[m * short : (m + 1) * short] = blocks[2 * other + 1 - near]


def edge_kernel(cols, quads, wide_ref, a_ref, b_ref, own_ref, inner_ref, outer_ref):
    bands, rows, _ = wide_ref.shape
    ext = rows + 2 * EDGE
    lane = lanes_of((ext, 128))
    quad = lax.axis_index("quad")
    left = jnp.zeros((ext, 128), F32)
    right = jnp.zeros((ext, 128), F32)
    for b in range(bands):
        halo = [
            pltpu.roll(ref[b // GROUP], (128 - (b % GROUP) * cols) % 128, 1)
            for ref in (a_ref, b_ref)
        ]
        north = jnp.where(quad > 0, halo[0], 0.0)
        south = jnp.where(quad < quads - 1, halo[1], 0.0)
        tile = jnp.concatenate([wide_ref[b], north, south], axis=0)
        own_ref[b] = tile
        at = RAD * b
        here = (lane >= at) & (lane < at + RAD)
        left = jnp.where(here, pltpu.roll(tile, at, 1), left)
        right = jnp.where(here, pltpu.roll(tile, (at - (cols - RAD)) % 128, 1), right)
    even = lax.axis_index("visit") % 2 == 0
    half = lane[: ext // 2] < 64
    for ref, edge in (
        (inner_ref, jnp.where(even, right, left)),
        (outer_ref, jnp.where(even, left, right)),
    ):
        ref[...] = jnp.where(half, edge[: ext // 2], pltpu.roll(edge[ext // 2 :], 64, 1))


def merge_kernel(rows, steps, mine_ref, got_ref, edge_ref, *out_refs):
    chips = len(out_refs) + 1
    short = rows // 2
    base = chips * short
    middle = edge_ref.shape[0]
    coefs = jnp.where(
        lanes_of((8, 128)) < 64,
        mine_ref[base : base + 8],
        pltpu.roll(got_ref[base : base + 8], 64, 1),
    )
    for m in range(1, chips):
        out_ref = out_refs[m - 1]
        at = slice(m * short, (m + 1) * short)
        out_ref[0:short] = mine_ref[at]
        out_ref[short:rows] = got_ref[at]
        out_ref[rows : rows + 8] = coefs
        if m in steps:
            out_ref[rows + 8 : rows + 8 + middle] = edge_ref[...]


def table_kernel(*refs):
    refs, sems = refs[1:-1], refs[-1]
    count = len(refs) // 2
    copies = [
        pltpu.make_async_copy(refs[i], refs[count + i], sems.at[i]) for i in range(count)
    ]
    for copy in copies:
        copy.start()
    for copy in copies:
        copy.wait()


def choose(which, tiles):
    shape = tiles[0].shape
    which = jnp.broadcast_to(which, shape)
    picked = jnp.zeros(shape, F32)
    for b, tile in enumerate(tiles):
        picked = jnp.where(which == float(b), tile, picked)
    return picked


def model_kernel(
    visits, quads, steps, mine_ref, got_ref, own_ref, inner_ref, tab_ref, dh_ref, dl_ref, *refs
):
    message_refs, (out_ref, near, stack, convs, fields) = refs[:-5], refs[-5:]
    bands, rows, cols = out_ref.shape
    short = rows // 2
    ext = rows + 2 * EDGE
    chips = visits // 2
    groups = visits // GROUP
    me = lax.axis_index("visit")
    quad = lax.axis_index("quad")
    chip = me // 2
    even = me % 2 == 0

    wide_lane = lanes_of((ext, 128))
    middle = ext // 2
    beside = jnp.where(even, chip - 1, chip + 1)
    exists = (beside >= 0) & (beside < chips)
    edge = jnp.zeros((middle, 128), F32)
    for m in steps:
        arrived = message_refs[m - 1][rows + 8 : rows + 8 + middle]
        edge = jnp.where(exists & ((chip ^ beside) == m), arrived, edge)
    outer, inner = [
        jnp.concatenate([part, pltpu.roll(part, 64, 1)], axis=0) for part in (edge, inner_ref[...])
    ]
    west = jnp.where(even, outer, inner)
    east = jnp.where(even, inner, outer)
    for b in range(bands):
        at = RAD * b
        tile = jnp.where(
            wide_lane < cols,
            own_ref[b],
            jnp.where(
                wide_lane < cols + RAD,
                pltpu.roll(west, (cols - at) % 128, 1),
                jnp.where(
                    wide_lane < cols + 2 * RAD,
                    pltpu.roll(east, (cols + RAD - at) % 128, 1),
                    0.0,
                ),
            ),
        )
        near[b] = jnp.where(wide_lane < 64, tile, pltpu.roll(tile, 64, 1))

    lane = lanes_of((rows, 128))
    flat = lane[:short]
    low_half = lane[:1] < 64
    x = (((lane % cols) + me * cols).astype(F32) + 0.5) / (visits * cols) * 2.0 - 1.0
    trow = lax.broadcasted_iota(jnp.int32, (rows, 256), 0)
    y = ((trow + quad * rows).astype(F32) + 0.5) / (quads * rows) * 2.0 - 1.0
    yy = y * y
    base = 8 * (lane // cols)
    base_row = chips * short
    slots = [
        (mine_ref, 0, mine_ref, base_row, False),
        (got_ref, 0, got_ref, base_row, False),
    ]
    for ref in message_refs:
        slots += [(ref, 0, ref, rows, False), (ref, short, ref, rows, True)]

    def gather(members):
        blocks, tails, band_rows = [], [], []
        for ref, at, tail_ref, tail_at, high in members:
            blocks.append(ref[at : at + short])
            tail = tail_ref[tail_at : tail_at + 8]
            turned = pltpu.roll(tail, 64, 1)
            tails.append(turned if high else tail)
            band_rows.append(jnp.where(low_half == (not high), tail[6:7], turned[6:7]))
        pieces = [jnp.zeros((short, 128), F32)] * 4
        which = jnp.zeros((1, 128), F32)
        for v in range(GROUP):
            here = (flat >= v * cols) & (flat < (v + 1) * cols)
            pieces = [
                jnp.where(here, pltpu.roll(blocks[v], (v * cols - 32 * k) % 128, 1), piece)
                for k, piece in enumerate(pieces)
            ]
            which = jnp.where(here[:1], band_rows[v], which)
        tails.append(jnp.zeros((128 - 8 * GROUP, 128), F32))
        cmat = jnp.transpose(jnp.concatenate(tails, axis=0))[0:rows]
        terms = [jnp.take_along_axis(cmat, base + s, axis=1) for s in range(6)]
        polys = (
            terms[0] + x * (terms[1] + x * terms[3]),
            terms[2] + x * terms[4],
            terms[5],
        )
        images = [
            choose(
                jnp.where(low_half, band_rows[2 * p], band_rows[2 * p + 1]),
                [near[b] for b in range(bands)],
            )
            for p in range(GROUP // 2)
        ]
        first = jnp.concatenate(pieces[:2], axis=0)
        second = jnp.concatenate(pieces[2:], axis=0)
        return polys, jnp.concatenate(images, axis=1), first, second, which

    totals = [jnp.zeros((rows, 128), F32) for _ in range(bands)]
    for start in range(0, groups, 2):
        pair = [gather(slots[g * GROUP : (g + 1) * GROUP]) for g in (start, start + 1)]
        parts = [split(image) for _, image, _, _, _ in pair]
        both = jnp.concatenate([p[0] for p in parts] + [p[1] for p in parts], axis=0)
        poly0, poly1, poly2 = [
            jnp.concatenate([pair[0][0][k], pair[1][0][k]], axis=1) for k in range(3)
        ]
        filt = 0
        for degree in DEGREES:
            count = degree + 1
            for j0 in range(0, count, 2):
                js = range(j0, min(j0 + 2, count))
                lanes = slice((filt + j0) * 128, (filt + js[-1] + 1) * 128)
                wide = jnp.dot(both, dh_ref[:, lanes], preferred_element_type=F32)
                conv = (
                    wide[: 2 * ext]
                    + wide[2 * ext :]
                    + jnp.dot(both[: 2 * ext], dl_ref[:, lanes], preferred_element_type=F32)
                )
                for j in js:
                    part = conv[:, (j - j0) * 128 : (j - j0 + 1) * 128]
                    high, low = split(jnp.concatenate([part[:ext], part[ext:]], axis=1))
                    at = (filt + j) * 3 * ext
                    stack[at : at + ext] = high
                    stack[at + ext : at + 2 * ext] = low
                    stack[at + 2 * ext : at + 3 * ext] = high
            filt += count
        basis_start = 0
        filt = 0
        for degree in DEGREES:
            count = degree + 1
            index = {}
            k = basis_start
            for i in range(count):
                for j in range(count - i):
                    index[i, j] = k
                    k += 1
            for j in range(count):
                at = (filt + j) * 3 * ext
                rowed = jnp.dot(
                    tab_ref[filt * rows : (filt + count - j) * rows],
                    stack[at : at + 3 * ext],
                    preferred_element_type=F32,
                )
                for i in range(count - j):
                    n = index[i, j]
                    convs[n * rows : (n + 1) * rows] = rowed[i * rows : (i + 1) * rows]
            basis_start = k
            filt += count
        for k, poly in enumerate((poly0, poly1, poly2)):
            fields[k] = poly
        pieces = []
        for at in range(0, rows, 8):
            level, square = y[at : at + 8], yy[at : at + 8]
            total = jnp.zeros((8, 256), F32)
            for n in range(basis_start):
                row = [fields[k, pl.ds(n, 8, stride=0), :] for k in range(3)]
                spatial = row[0] + level * row[1] + square * row[2]
                total = total + spatial * convs[n * rows + at : n * rows + at + 8]
            pieces.append(total)
        model = jnp.concatenate(pieces, axis=0)
        for g in range(2):
            _, _, first, second, which = pair[g]
            part = first - second * model[:, g * 128 : (g + 1) * 128]
            which = jnp.broadcast_to(which, (rows, 128))
            for b in range(bands):
                totals[b] = totals[b] + jnp.where(which == float(b), part, 0.0)
    for b in range(bands):
        folded = totals[b] + pltpu.roll(totals[b], 64, 1)
        out_ref[b] = (folded + pltpu.roll(folded, 96, 1))[:, 0:cols]


def swaps(count, start):
    pairs = [(i, i + 1) for i in range(start, count - 1, 2)]
    return pairs + [(j, i) for i, j in pairs]


def stay(array):
    return pltpu.with_memory_space_constraint(array, pltpu.HBM)


def per_device(template, science, variance, coeffs, visit_weight, band, footprint):
    visits, quads = lax.axis_size("visit"), lax.axis_size("quad")
    chips = visits // 2
    bands, rows, cols = template.shape
    ext = rows + 2 * EDGE
    short = rows // 2
    vmem = pl.BlockSpec(memory_space=pltpu.VMEM)
    hbm = pl.BlockSpec(memory_space=pltpu.HBM)
    params = pltpu.CompilerParams(vmem_limit_bytes=24 * 1024 * 1024)
    struct = jax.ShapeDtypeStruct

    def call(kernel, outs, ins, scratch=(), params=params):
        return pl.pallas_call(
            kernel,
            out_shape=outs,
            in_specs=ins,
            out_specs=jax.tree.map(lambda _: vmem, outs),
            scratch_shapes=scratch,
            compiler_params=params,
        )

    turned = jnp.transpose(coeffs, (2, 0, 1))
    sources = [stay(array) for array in (template, science, variance, turned, footprint)]
    strip = struct((-(-bands // GROUP), EDGE, 128), F32)
    first, second, wide, *loaded = call(
        functools.partial(load_kernel, len(sources)),
        [strip, strip, struct((bands, rows, 128), F32)]
        + [struct(a.shape, a.dtype) for a in sources[1:]],
        [hbm] * 5,
        [pltpu.VMEM(template.shape, F32), pltpu.SemaphoreType.DMA((5,))],
    )(*sources)
    halo_a = lax.ppermute(first, "quad", [(i, (i + 1) % quads) for i in range(quads)])
    halo_b = lax.ppermute(second, "quad", [((i + 1) % quads, i) for i in range(quads)])
    height = chips * short + 8
    mine, away = call(
        functools.partial(pack_kernel, visits, cols),
        [struct((height, 128), F32)] * 2,
        [vmem] * 4 + [pl.BlockSpec(memory_space=pltpu.SMEM)] * 2,
        [pltpu.VMEM((visits, short, 128), F32)],
    )(*loaded, visit_weight, band)
    got = lax.ppermute(away, "visit", swaps(visits, 0))
    own, to_core, to_chips = call(
        functools.partial(edge_kernel, cols, quads),
        [struct((bands, ext, 128), F32)] + [struct((ext // 2, 128), F32)] * 2,
        [vmem] * 3,
    )(wide, halo_a, halo_b)
    edge = lax.ppermute(to_core, "visit", swaps(visits, 0))
    steps = sorted({c ^ (c + 1) for c in range(chips - 1)})
    outgoing = call(
        functools.partial(merge_kernel, rows, steps),
        [
            struct((rows + 8 + (ext // 2 if m in steps else 0), 128), F32)
            for m in range(1, chips)
        ],
        [vmem] * 3,
    )(mine, got, to_chips)
    incoming = [
        lax.ppermute(array, "visit", [(i, i ^ (2 * m + 1)) for i in range(visits)])
        for m, array in enumerate(outgoing, 1)
    ]
    tables = [
        stay(jnp.asarray(array)) for array in (row_weights(rows),) + column_weights(cols, 64)
    ]
    tables = call(
        table_kernel,
        [struct(a.shape, a.dtype) for a in tables],
        [vmem] + [hbm] * 3,
        [pltpu.SemaphoreType.DMA((3,))],
    )(outgoing[0], *tables)
    return call(
        functools.partial(model_kernel, visits, quads, steps),
        struct((bands, rows, cols), F32),
        [vmem] * (7 + chips - 1),
        [pltpu.VMEM((bands, ext, 128), F32), pltpu.VMEM((12 * 3 * ext, 256), BF16), pltpu.VMEM((coeffs.shape[1] * rows, 256), F32), pltpu.VMEM((3, rows, 256), F32)],
        params=pltpu.CompilerParams(vmem_limit_bytes=24 * 1024 * 1024),
    )(mine, got, own, edge, *tables, *incoming)


def solution(mesh):
    placed = (
        P(None, "quad", "visit"),
        P("visit", "quad", None),
        P("visit", "quad", None),
        P("visit", None, None),
        P("visit"),
        P("visit"),
        P("visit", "quad", None),
    )
    return jax.shard_map(
        per_device, mesh=mesh, in_specs=placed, out_specs=P(None, "quad", "visit"), check_vma=False
    )
```

```python
import functools

import jax
import jax.numpy as jnp
import numpy as np
from jax import lax
from jax.experimental import pallas as pl
from jax.experimental.pallas import tpu as pltpu
from jax.sharding import PartitionSpec as P


RAD = 10
EDGE = 16
SIGMAS = (1.0, 2.5, 5.0)
DEGREES = (4, 3, 2)
GROUP = 4
F32 = jnp.float32
BF16 = jnp.bfloat16


def taps(sigma, power):
    offsets = np.arange(-RAD, RAD + 1).astype(np.float64)
    bell = np.exp(-offsets * offsets / (2.0 * sigma * sigma))
    return bell / bell.sum() * (offsets / sigma) ** power


def band_matrix(positions, outs):
    tables = []
    for sigma, degree in zip(SIGMAS, DEGREES):
        for power in range(degree + 1):
            filt = taps(sigma, power)
            offset = positions[None, :] - np.arange(outs)[:, None]
            inside = np.abs(offset) <= RAD
            tables.append(np.where(inside, filt[np.clip(offset + RAD, 0, 2 * RAD)], 0.0))
    return np.stack(tables).astype(np.float32)


def split(array):
    high = array.astype(BF16)
    low = (array.astype(F32) - high.astype(F32)).astype(BF16)
    return high, low


def np_split(array):
    high = array.astype(jnp.bfloat16)
    low = (array - high.astype(np.float32)).astype(jnp.bfloat16)
    return high, low


def row_weights(rows):
    positions = np.concatenate(
        [np.arange(rows), np.arange(EDGE) - EDGE, rows + np.arange(EDGE)]
    )
    table = band_matrix(positions, rows).reshape(-1, rows + 2 * EDGE)
    high, low = np_split(table)
    return np.concatenate([high, high, low], axis=1)


def column_weights(cols, lanes):
    far = 10 * cols + 1000
    positions = np.concatenate(
        [
            np.arange(cols),
            np.arange(RAD) - RAD,
            cols + np.arange(RAD),
            np.full(lanes - cols - 2 * RAD, far),
        ]
    )
    table = band_matrix(positions, cols)
    count = table.shape[0]
    wide = np.zeros((GROUP, lanes, count, GROUP, cols), np.float32)
    for v in range(GROUP):
        wide[v, :, :, v, :] = table.transpose(2, 0, 1)
    return np_split(wide.reshape(GROUP * lanes, count * GROUP * cols))


def lanes_of(shape):
    return lax.broadcasted_iota(jnp.int32, shape, 1)


def packed(tiles, cols):
    lane = lanes_of(tiles[0].shape)
    out = []
    for b in range(0, len(tiles), GROUP):
        tile = tiles[b]
        for k in range(1, min(GROUP, len(tiles) - b)):
            tile = jnp.where(lane < k * cols, tile, pltpu.roll(tiles[b + k], k * cols, 1))
        out.append(tile)
    return out


def load_kernel(count, *refs):
    sources, refs = refs[:count], refs[count:]
    (first_ref, second_ref, wide_ref), refs = refs[:3], refs[3:]
    targets, (t_ref, sems) = refs[: count - 1], refs[count - 1 :]
    copies = [
        pltpu.make_async_copy(a, b, sems.at[i])
        for i, (a, b) in enumerate(zip(sources, (t_ref, *targets)))
    ]
    for copy in copies:
        copy.start()
    copies[0].wait()
    bands, rows, cols = t_ref.shape
    wide_ref[:, :, 0:cols] = t_ref[...]
    for k, tile in enumerate(packed([wide_ref[b] for b in range(bands)], cols)):
        last, leading = tile[rows - EDGE :], tile[:EDGE]
        first_ref[k] = last
        second_ref[k] = leading
    for copy in copies[1:]:
        copy.wait()


def pack_kernel(
    visits, cols, sci_ref, var_ref, coef_ref, foot_ref, w_ref, band_ref, mine_ref, away_ref, blocks
):
    rows = sci_ref.shape[1]
    short = rows // 2
    chips = visits // 2
    me = lax.axis_index("visit")
    chip, side = me // 2, me % 2
    at = chips * short
    weight = w_ref[0]
    coef = coef_ref[:, 0, :]
    terms, basis = coef.shape
    which = jnp.full((1, 128), band_ref[0].astype(F32), F32)
    for ref in (mine_ref, away_ref):
        ref[at : at + terms, 0:basis] = coef
        ref[at + terms : at + terms + 1] = which
    tile_rows, tile_cols = foot_ref.shape[1], foot_ref.shape[2]
    foot = foot_ref[0].astype(F32)
    width = sci_ref.shape[2]
    height = rows // tile_rows
    span = width // tile_cols
    per = 128 // span
    tcol = lax.broadcasted_iota(jnp.int32, (tile_cols, 128), 0)
    tlane = lanes_of((tile_cols, 128)) // span
    parts = []
    for chunk in range(width // 128):
        pick = jnp.where(tcol == tlane + chunk * per, 1.0, 0.0).astype(F32)
        cover = jnp.dot(foot, pick, preferred_element_type=F32)
        cover = jnp.concatenate(
            [jnp.broadcast_to(cover[k : k + 1], (height, 128)) for k in range(tile_rows)], axis=0
        )
        inside = slice(chunk * 128, chunk * 128 + 128)
        scale = weight * cover / var_ref[0, :, inside]
        parts.append((scale * sci_ref[0, :, inside], scale))
    flat = lanes_of((short, 128))
    for d in range(visits):
        whole, within = (d * cols) // 128, (d * cols) % 128
        first, second = parts[whole]
        pieces = (first[:short], first[short:], second[:short], second[short:])
        block = pltpu.roll(pieces[0], (128 - within) % 128, 1)
        for k in range(1, 4):
            turned = pltpu.roll(pieces[k], (128 + 32 * k - within) % 128, 1)
            block = jnp.where(flat < 32 * k, block, turned)
        blocks[d] = block
    for m in range(chips):
        near = side if m == 0 else 1 - side
        other = chip ^ m
        mine_ref[m * short : (m + 1) * short] = blocks[2 * other + near]
        away_ref[m * short : (m + 1) * short] = blocks[2 * other + 1 - near]


def edge_kernel(cols, quads, wide_ref, a_ref, b_ref, own_ref, inner_ref, outer_ref):
    bands, rows, _ = wide_ref.shape
    ext = rows + 2 * EDGE
    lane = lanes_of((ext, 128))
    quad = lax.axis_index("quad")
    left = jnp.zeros((ext, 128), F32)
    right = jnp.zeros((ext, 128), F32)
    for b in range(bands):
        halo = [
            pltpu.roll(ref[b // GROUP], (128 - (b % GROUP) * cols) % 128, 1)
            for ref in (a_ref, b_ref)
        ]
        north = jnp.where(quad > 0, halo[0], 0.0)
        south = jnp.where(quad < quads - 1, halo[1], 0.0)
        tile = jnp.concatenate([wide_ref[b], north, south], axis=0)
        own_ref[b] = tile
        at = RAD * b
        here = (lane >= at) & (lane < at + RAD)
        left = jnp.where(here, pltpu.roll(tile, at, 1), left)
        right = jnp.where(here, pltpu.roll(tile, (at - (cols - RAD)) % 128, 1), right)
    even = lax.axis_index("visit") % 2 == 0
    half = lane[: ext // 2] < 64
    for ref, edge in (
        (inner_ref, jnp.where(even, right, left)),
        (outer_ref, jnp.where(even, left, right)),
    ):
        ref[...] = jnp.where(half, edge[: ext // 2], pltpu.roll(edge[ext // 2 :], 64, 1))


def merge_kernel(rows, steps, mine_ref, got_ref, edge_ref, *out_refs):
    chips = len(out_refs) + 1
    short = rows // 2
    base = chips * short
    middle = edge_ref.shape[0]
    coefs = jnp.where(
        lanes_of((8, 128)) < 64,
        mine_ref[base : base + 8],
        pltpu.roll(got_ref[base : base + 8], 64, 1),
    )
    for m in range(1, chips):
        out_ref = out_refs[m - 1]
        at = slice(m * short, (m + 1) * short)
        out_ref[0:short] = mine_ref[at]
        out_ref[short:rows] = got_ref[at]
        out_ref[rows : rows + 8] = coefs
        if m in steps:
            out_ref[rows + 8 : rows + 8 + middle] = edge_ref[...]


def table_kernel(*refs):
    refs, sems = refs[1:-1], refs[-1]
    count = len(refs) // 2
    copies = [
        pltpu.make_async_copy(refs[i], refs[count + i], sems.at[i]) for i in range(count)
    ]
    for copy in copies:
        copy.start()
    for copy in copies:
        copy.wait()


def choose(which, tiles):
    shape = tiles[0].shape
    which = jnp.broadcast_to(which, shape)
    picked = jnp.zeros(shape, F32)
    for b, tile in enumerate(tiles):
        picked = jnp.where(which == float(b), tile, picked)
    return picked


def model_kernel(
    visits, quads, steps, mine_ref, got_ref, own_ref, inner_ref, tab_ref, dh_ref, dl_ref, *refs
):
    message_refs, (out_ref, near, stack) = refs[:-3], refs[-3:]
    bands, rows, cols = out_ref.shape
    short = rows // 2
    ext = rows + 2 * EDGE
    chips = visits // 2
    groups = visits // GROUP
    me = lax.axis_index("visit")
    quad = lax.axis_index("quad")
    chip = me // 2
    even = me % 2 == 0

    wide_lane = lanes_of((ext, 128))
    middle = ext // 2
    beside = jnp.where(even, chip - 1, chip + 1)
    exists = (beside >= 0) & (beside < chips)
    edge = jnp.zeros((middle, 128), F32)
    for m in steps:
        arrived = message_refs[m - 1][rows + 8 : rows + 8 + middle]
        edge = jnp.where(exists & ((chip ^ beside) == m), arrived, edge)
    outer, inner = [
        jnp.concatenate([part, pltpu.roll(part, 64, 1)], axis=0) for part in (edge, inner_ref[...])
    ]
    west = jnp.where(even, outer, inner)
    east = jnp.where(even, inner, outer)
    for b in range(bands):
        at = RAD * b
        tile = jnp.where(
            wide_lane < cols,
            own_ref[b],
            jnp.where(
                wide_lane < cols + RAD,
                pltpu.roll(west, (cols - at) % 128, 1),
                jnp.where(
                    wide_lane < cols + 2 * RAD,
                    pltpu.roll(east, (cols + RAD - at) % 128, 1),
                    0.0,
                ),
            ),
        )
        near[b] = jnp.where(wide_lane < 64, tile, pltpu.roll(tile, 64, 1))

    lane = lanes_of((rows, 128))
    flat = lane[:short]
    low_half = lane[:1] < 64
    x = (((lane % cols) + me * cols).astype(F32) + 0.5) / (visits * cols) * 2.0 - 1.0
    trow = lax.broadcasted_iota(jnp.int32, (rows, 256), 0)
    y = ((trow + quad * rows).astype(F32) + 0.5) / (quads * rows) * 2.0 - 1.0
    yy = y * y
    base = 8 * (lane // cols)
    base_row = chips * short
    slots = [
        (mine_ref, 0, mine_ref, base_row, False),
        (got_ref, 0, got_ref, base_row, False),
    ]
    for ref in message_refs:
        slots += [(ref, 0, ref, rows, False), (ref, short, ref, rows, True)]

    def gather(members):
        blocks, tails, band_rows = [], [], []
        for ref, at, tail_ref, tail_at, high in members:
            blocks.append(ref[at : at + short])
            tail = tail_ref[tail_at : tail_at + 8]
            turned = pltpu.roll(tail, 64, 1)
            tails.append(turned if high else tail)
            band_rows.append(jnp.where(low_half == (not high), tail[6:7], turned[6:7]))
        pieces = [jnp.zeros((short, 128), F32)] * 4
        which = jnp.zeros((1, 128), F32)
        for v in range(GROUP):
            here = (flat >= v * cols) & (flat < (v + 1) * cols)
            pieces = [
                jnp.where(here, pltpu.roll(blocks[v], (v * cols - 32 * k) % 128, 1), piece)
                for k, piece in enumerate(pieces)
            ]
            which = jnp.where(here[:1], band_rows[v], which)
        tails.append(jnp.zeros((128 - 8 * GROUP, 128), F32))
        cmat = jnp.transpose(jnp.concatenate(tails, axis=0))[0:rows]
        terms = [jnp.take_along_axis(cmat, base + s, axis=1) for s in range(6)]
        polys = (
            terms[0] + x * (terms[1] + x * terms[3]),
            terms[2] + x * terms[4],
            terms[5],
        )
        images = [
            choose(
                jnp.where(low_half, band_rows[2 * p], band_rows[2 * p + 1]),
                [near[b] for b in range(bands)],
            )
            for p in range(GROUP // 2)
        ]
        first = jnp.concatenate(pieces[:2], axis=0)
        second = jnp.concatenate(pieces[2:], axis=0)
        return polys, jnp.concatenate(images, axis=1), first, second, which

    totals = [jnp.zeros((rows, 128), F32) for _ in range(bands)]
    for start in range(0, groups, 2):
        pair = [gather(slots[g * GROUP : (g + 1) * GROUP]) for g in (start, start + 1)]
        parts = [split(image) for _, image, _, _, _ in pair]
        both = jnp.concatenate([p[0] for p in parts] + [p[1] for p in parts], axis=0)
        poly0, poly1, poly2 = [
            jnp.concatenate([pair[0][0][k], pair[1][0][k]], axis=1) for k in range(3)
        ]
        filt = 0
        for degree in DEGREES:
            count = degree + 1
            for j0 in range(0, count, 2):
                js = range(j0, min(j0 + 2, count))
                lanes = slice((filt + j0) * 128, (filt + js[-1] + 1) * 128)
                wide = jnp.dot(both, dh_ref[:, lanes], preferred_element_type=F32)
                conv = (
                    wide[: 2 * ext]
                    + wide[2 * ext :]
                    + jnp.dot(both[: 2 * ext], dl_ref[:, lanes], preferred_element_type=F32)
                )
                for j in js:
                    part = conv[:, (j - j0) * 128 : (j - j0 + 1) * 128]
                    high, low = split(jnp.concatenate([part[:ext], part[ext:]], axis=1))
                    at = (filt + j) * 3 * ext
                    stack[at : at + ext] = high
                    stack[at + ext : at + 2 * ext] = low
                    stack[at + 2 * ext : at + 3 * ext] = high
            filt += count
        model = jnp.zeros((rows, 256), F32)
        basis_start = 0
        filt = 0
        for degree in DEGREES:
            count = degree + 1
            index = {}
            k = basis_start
            for i in range(count):
                for j in range(count - i):
                    index[i, j] = k
                    k += 1
            for j in range(count):
                at = (filt + j) * 3 * ext
                rowed = jnp.dot(
                    tab_ref[filt * rows : (filt + count - j) * rows],
                    stack[at : at + 3 * ext],
                    preferred_element_type=F32,
                )
                for i in range(count - j):
                    n = index[i, j]
                    spatial = poly0[n : n + 1] + y * poly1[n : n + 1] + yy * poly2[n : n + 1]
                    model = model + spatial * rowed[i * rows : (i + 1) * rows]
            basis_start = k
            filt += count
        for g in range(2):
            _, _, first, second, which = pair[g]
            part = first - second * model[:, g * 128 : (g + 1) * 128]
            which = jnp.broadcast_to(which, (rows, 128))
            for b in range(bands):
                totals[b] = totals[b] + jnp.where(which == float(b), part, 0.0)
    for b in range(bands):
        folded = totals[b] + pltpu.roll(totals[b], 64, 1)
        out_ref[b] = (folded + pltpu.roll(folded, 96, 1))[:, 0:cols]


def swaps(count, start):
    pairs = [(i, i + 1) for i in range(start, count - 1, 2)]
    return pairs + [(j, i) for i, j in pairs]


def stay(array):
    return pltpu.with_memory_space_constraint(array, pltpu.HBM)


def per_device(template, science, variance, coeffs, visit_weight, band, footprint):
    visits, quads = lax.axis_size("visit"), lax.axis_size("quad")
    chips = visits // 2
    bands, rows, cols = template.shape
    ext = rows + 2 * EDGE
    short = rows // 2
    vmem = pl.BlockSpec(memory_space=pltpu.VMEM)
    hbm = pl.BlockSpec(memory_space=pltpu.HBM)
    params = pltpu.CompilerParams(vmem_limit_bytes=24 * 1024 * 1024)
    struct = jax.ShapeDtypeStruct

    def call(kernel, outs, ins, scratch=()):
        return pl.pallas_call(
            kernel,
            out_shape=outs,
            in_specs=ins,
            out_specs=jax.tree.map(lambda _: vmem, outs),
            scratch_shapes=scratch,
            compiler_params=params,
        )

    turned = jnp.transpose(coeffs, (2, 0, 1))
    sources = [stay(array) for array in (template, science, variance, turned, footprint)]
    strip = struct((-(-bands // GROUP), EDGE, 128), F32)
    first, second, wide, *loaded = call(
        functools.partial(load_kernel, len(sources)),
        [strip, strip, struct((bands, rows, 128), F32)]
        + [struct(a.shape, a.dtype) for a in sources[1:]],
        [hbm] * 5,
        [pltpu.VMEM(template.shape, F32), pltpu.SemaphoreType.DMA((5,))],
    )(*sources)
    halo_a = lax.ppermute(first, "quad", [(i, (i + 1) % quads) for i in range(quads)])
    halo_b = lax.ppermute(second, "quad", [((i + 1) % quads, i) for i in range(quads)])
    height = chips * short + 8
    mine, away = call(
        functools.partial(pack_kernel, visits, cols),
        [struct((height, 128), F32)] * 2,
        [vmem] * 4 + [pl.BlockSpec(memory_space=pltpu.SMEM)] * 2,
        [pltpu.VMEM((visits, short, 128), F32)],
    )(*loaded, visit_weight, band)
    got = lax.ppermute(away, "visit", swaps(visits, 0))
    own, to_core, to_chips = call(
        functools.partial(edge_kernel, cols, quads),
        [struct((bands, ext, 128), F32)] + [struct((ext // 2, 128), F32)] * 2,
        [vmem] * 3,
    )(wide, halo_a, halo_b)
    edge = lax.ppermute(to_core, "visit", swaps(visits, 0))
    steps = sorted({c ^ (c + 1) for c in range(chips - 1)})
    outgoing = call(
        functools.partial(merge_kernel, rows, steps),
        [
            struct((rows + 8 + (ext // 2 if m in steps else 0), 128), F32)
            for m in range(1, chips)
        ],
        [vmem] * 3,
    )(mine, got, to_chips)
    incoming = [
        lax.ppermute(array, "visit", [(i, i ^ (2 * m + 1)) for i in range(visits)])
        for m, array in enumerate(outgoing, 1)
    ]
    tables = [
        stay(jnp.asarray(array)) for array in (row_weights(rows),) + column_weights(cols, 64)
    ]
    tables = call(
        table_kernel,
        [struct(a.shape, a.dtype) for a in tables],
        [vmem] + [hbm] * 3,
        [pltpu.SemaphoreType.DMA((3,))],
    )(outgoing[0], *tables)
    return call(
        functools.partial(model_kernel, visits, quads, steps),
        struct((bands, rows, cols), F32),
        [vmem] * (7 + chips - 1),
        [pltpu.VMEM((bands, ext, 128), F32), pltpu.VMEM((12 * 3 * ext, 256), BF16)],
    )(mine, got, own, edge, *tables, *incoming)


def solution(mesh):
    placed = (
        P(None, "quad", "visit"),
        P("visit", "quad", None),
        P("visit", "quad", None),
        P("visit", None, None),
        P("visit"),
        P("visit"),
        P("visit", "quad", None),
    )
    return jax.shard_map(
        per_device, mesh=mesh, in_specs=placed, out_specs=P(None, "quad", "visit"), check_vma=False
    )
```

```python
import functools

import jax
import jax.numpy as jnp
import numpy as np
from jax import lax
from jax.experimental import pallas as pl
from jax.experimental.pallas import tpu as pltpu
from jax.sharding import PartitionSpec as P


RAD = 10
EDGE = 16
SIGMAS = (1.0, 2.5, 5.0)
DEGREES = (4, 3, 2)
GROUP = 4
F32 = jnp.float32
BF16 = jnp.bfloat16


def taps(sigma, power):
    offsets = np.arange(-RAD, RAD + 1).astype(np.float64)
    bell = np.exp(-offsets * offsets / (2.0 * sigma * sigma))
    return bell / bell.sum() * (offsets / sigma) ** power


def band_matrix(positions, outs):
    tables = []
    for sigma, degree in zip(SIGMAS, DEGREES):
        for power in range(degree + 1):
            filt = taps(sigma, power)
            offset = positions[None, :] - np.arange(outs)[:, None]
            inside = np.abs(offset) <= RAD
            tables.append(np.where(inside, filt[np.clip(offset + RAD, 0, 2 * RAD)], 0.0))
    return np.stack(tables).astype(np.float32)


def split(array):
    high = array.astype(BF16)
    low = (array.astype(F32) - high.astype(F32)).astype(BF16)
    return high, low


def np_split(array):
    high = array.astype(jnp.bfloat16)
    low = (array - high.astype(np.float32)).astype(jnp.bfloat16)
    return high, low


def row_weights(rows):
    positions = np.concatenate(
        [np.arange(rows), np.arange(EDGE) - EDGE, rows + np.arange(EDGE)]
    )
    table = band_matrix(positions, rows).reshape(-1, rows + 2 * EDGE)
    high, low = np_split(table)
    return np.concatenate([high, high, low], axis=1)


def column_weights(cols, lanes):
    far = 10 * cols + 1000
    positions = np.concatenate(
        [
            np.arange(cols),
            np.arange(RAD) - RAD,
            cols + np.arange(RAD),
            np.full(lanes - cols - 2 * RAD, far),
        ]
    )
    table = band_matrix(positions, cols)
    count = table.shape[0]
    wide = np.zeros((GROUP, lanes, count, GROUP, cols), np.float32)
    for v in range(GROUP):
        wide[v, :, :, v, :] = table.transpose(2, 0, 1)
    return np_split(wide.reshape(GROUP * lanes, count * GROUP * cols))


def lanes_of(shape):
    return lax.broadcasted_iota(jnp.int32, shape, 1)


def packed(tiles, cols):
    lane = lanes_of(tiles[0].shape)
    out = []
    for b in range(0, len(tiles), GROUP):
        tile = tiles[b]
        for k in range(1, min(GROUP, len(tiles) - b)):
            tile = jnp.where(lane < k * cols, tile, pltpu.roll(tiles[b + k], k * cols, 1))
        out.append(tile)
    return out


def load_kernel(count, *refs):
    sources, refs = refs[:count], refs[count:]
    (first_ref, second_ref, wide_ref), refs = refs[:3], refs[3:]
    targets, (t_ref, sems) = refs[: count - 1], refs[count - 1 :]
    copies = [
        pltpu.make_async_copy(a, b, sems.at[i])
        for i, (a, b) in enumerate(zip(sources, (t_ref, *targets)))
    ]
    for copy in copies:
        copy.start()
    copies[0].wait()
    bands, rows, cols = t_ref.shape
    wide_ref[:, :, 0:cols] = t_ref[...]
    for k, tile in enumerate(packed([wide_ref[b] for b in range(bands)], cols)):
        last, leading = tile[rows - EDGE :], tile[:EDGE]
        first_ref[k] = last
        second_ref[k] = leading
    for copy in copies[1:]:
        copy.wait()


def pack_kernel(
    visits, cols, sci_ref, var_ref, coef_ref, foot_ref, w_ref, band_ref, mine_ref, away_ref, blocks
):
    rows = sci_ref.shape[1]
    short = rows // 2
    chips = visits // 2
    me = lax.axis_index("visit")
    chip, side = me // 2, me % 2
    at = chips * short
    weight = w_ref[0]
    coef = coef_ref[:, 0, :]
    terms, basis = coef.shape
    which = jnp.full((1, 128), band_ref[0].astype(F32), F32)
    for ref in (mine_ref, away_ref):
        ref[at : at + terms, 0:basis] = coef
        ref[at + terms : at + terms + 1] = which
    tile_rows, tile_cols = foot_ref.shape[1], foot_ref.shape[2]
    foot = foot_ref[0].astype(F32)
    width = sci_ref.shape[2]
    height = rows // tile_rows
    span = width // tile_cols
    per = 128 // span
    tcol = lax.broadcasted_iota(jnp.int32, (tile_cols, 128), 0)
    tlane = lanes_of((tile_cols, 128)) // span
    parts = []
    for chunk in range(width // 128):
        pick = jnp.where(tcol == tlane + chunk * per, 1.0, 0.0).astype(F32)
        cover = jnp.dot(foot, pick, preferred_element_type=F32)
        cover = jnp.concatenate(
            [jnp.broadcast_to(cover[k : k + 1], (height, 128)) for k in range(tile_rows)], axis=0
        )
        inside = slice(chunk * 128, chunk * 128 + 128)
        scale = weight * cover / var_ref[0, :, inside]
        parts.append((scale * sci_ref[0, :, inside], scale))
    flat = lanes_of((short, 128))
    for d in range(visits):
        whole, within = (d * cols) // 128, (d * cols) % 128
        first, second = parts[whole]
        pieces = (first[:short], first[short:], second[:short], second[short:])
        block = pltpu.roll(pieces[0], (128 - within) % 128, 1)
        for k in range(1, 4):
            turned = pltpu.roll(pieces[k], (128 + 32 * k - within) % 128, 1)
            block = jnp.where(flat < 32 * k, block, turned)
        blocks[d] = block
    for m in range(chips):
        near = side if m == 0 else 1 - side
        other = chip ^ m
        mine_ref[m * short : (m + 1) * short] = blocks[2 * other + near]
        away_ref[m * short : (m + 1) * short] = blocks[2 * other + 1 - near]


def edge_kernel(cols, quads, wide_ref, a_ref, b_ref, own_ref, inner_ref, outer_ref):
    bands, rows, _ = wide_ref.shape
    ext = rows + 2 * EDGE
    lane = lanes_of((ext, 128))
    quad = lax.axis_index("quad")
    left = jnp.zeros((ext, 128), F32)
    right = jnp.zeros((ext, 128), F32)
    for b in range(bands):
        halo = [
            pltpu.roll(ref[b // GROUP], (128 - (b % GROUP) * cols) % 128, 1)
            for ref in (a_ref, b_ref)
        ]
        north = jnp.where(quad > 0, halo[0], 0.0)
        south = jnp.where(quad < quads - 1, halo[1], 0.0)
        tile = jnp.concatenate([wide_ref[b], north, south], axis=0)
        own_ref[b] = tile
        at = RAD * b
        here = (lane >= at) & (lane < at + RAD)
        left = jnp.where(here, pltpu.roll(tile, at, 1), left)
        right = jnp.where(here, pltpu.roll(tile, (at - (cols - RAD)) % 128, 1), right)
    even = lax.axis_index("visit") % 2 == 0
    half = lane[: ext // 2] < 64
    for ref, edge in (
        (inner_ref, jnp.where(even, right, left)),
        (outer_ref, jnp.where(even, left, right)),
    ):
        ref[...] = jnp.where(half, edge[: ext // 2], pltpu.roll(edge[ext // 2 :], 64, 1))


def merge_kernel(rows, steps, mine_ref, got_ref, edge_ref, *out_refs):
    chips = len(out_refs) + 1
    short = rows // 2
    base = chips * short
    middle = edge_ref.shape[0]
    coefs = jnp.where(
        lanes_of((8, 128)) < 64,
        mine_ref[base : base + 8],
        pltpu.roll(got_ref[base : base + 8], 64, 1),
    )
    for m in range(1, chips):
        out_ref = out_refs[m - 1]
        at = slice(m * short, (m + 1) * short)
        out_ref[0:short] = mine_ref[at]
        out_ref[short:rows] = got_ref[at]
        out_ref[rows : rows + 8] = coefs
        if m in steps:
            out_ref[rows + 8 : rows + 8 + middle] = edge_ref[...]


def table_kernel(*refs):
    refs, sems = refs[1:-1], refs[-1]
    count = len(refs) // 2
    copies = [
        pltpu.make_async_copy(refs[i], refs[count + i], sems.at[i]) for i in range(count)
    ]
    for copy in copies:
        copy.start()
    for copy in copies:
        copy.wait()


def choose(which, tiles):
    shape = tiles[0].shape
    which = jnp.broadcast_to(which, shape)
    picked = jnp.zeros(shape, F32)
    for b, tile in enumerate(tiles):
        picked = jnp.where(which == float(b), tile, picked)
    return picked


def model_kernel(
    visits, quads, steps, mine_ref, got_ref, own_ref, inner_ref, tab_ref, dh_ref, dl_ref, *refs
):
    message_refs, (out_ref, near, stack) = refs[:-3], refs[-3:]
    bands, rows, cols = out_ref.shape
    short = rows // 2
    ext = rows + 2 * EDGE
    chips = visits // 2
    groups = visits // GROUP
    me = lax.axis_index("visit")
    quad = lax.axis_index("quad")
    chip = me // 2
    even = me % 2 == 0

    wide_lane = lanes_of((ext, 128))
    middle = ext // 2
    beside = jnp.where(even, chip - 1, chip + 1)
    exists = (beside >= 0) & (beside < chips)
    edge = jnp.zeros((middle, 128), F32)
    for m in steps:
        arrived = message_refs[m - 1][rows + 8 : rows + 8 + middle]
        edge = jnp.where(exists & ((chip ^ beside) == m), arrived, edge)
    outer, inner = [
        jnp.concatenate([part, pltpu.roll(part, 64, 1)], axis=0) for part in (edge, inner_ref[...])
    ]
    west = jnp.where(even, outer, inner)
    east = jnp.where(even, inner, outer)
    for b in range(bands):
        at = RAD * b
        tile = jnp.where(
            wide_lane < cols,
            own_ref[b],
            jnp.where(
                wide_lane < cols + RAD,
                pltpu.roll(west, (cols - at) % 128, 1),
                jnp.where(
                    wide_lane < cols + 2 * RAD,
                    pltpu.roll(east, (cols + RAD - at) % 128, 1),
                    0.0,
                ),
            ),
        )
        near[b] = jnp.where(wide_lane < 64, tile, pltpu.roll(tile, 64, 1))

    lane = lanes_of((rows, 128))
    flat = lane[:short]
    low_half = lane[:1] < 64
    x = (((lane % cols) + me * cols).astype(F32) + 0.5) / (visits * cols) * 2.0 - 1.0
    trow = lax.broadcasted_iota(jnp.int32, (rows, 256), 0)
    y = ((trow + quad * rows).astype(F32) + 0.5) / (quads * rows) * 2.0 - 1.0
    yy = y * y
    base = 8 * (lane // cols)
    base_row = chips * short
    slots = [
        (mine_ref, 0, mine_ref, base_row, False),
        (got_ref, 0, got_ref, base_row, False),
    ]
    for ref in message_refs:
        slots += [(ref, 0, ref, rows, False), (ref, short, ref, rows, True)]

    def select(members):
        tails, band_rows = [], []
        for _, _, tail_ref, tail_at, high in members:
            tail = tail_ref[tail_at : tail_at + 8]
            turned = pltpu.roll(tail, 64, 1)
            tails.append(turned if high else tail)
            band_rows.append(jnp.where(low_half == (not high), tail[6:7], turned[6:7]))
        images = [
            choose(
                jnp.where(low_half, band_rows[2 * p], band_rows[2 * p + 1]),
                [near[b] for b in range(bands)],
            )
            for p in range(GROUP // 2)
        ]
        return jnp.concatenate(images, axis=1), tails, band_rows

    def gather(members, tails, band_rows):
        pieces = [jnp.zeros((short, 128), F32)] * 4
        which = jnp.zeros((1, 128), F32)
        for v, (ref, at, _, _, _) in enumerate(members):
            block = ref[at : at + short]
            here = (flat >= v * cols) & (flat < (v + 1) * cols)
            pieces = [
                jnp.where(here, pltpu.roll(block, (v * cols - 32 * k) % 128, 1), piece)
                for k, piece in enumerate(pieces)
            ]
            which = jnp.where(here[:1], band_rows[v], which)
        padded = tails + [jnp.zeros((128 - 8 * GROUP, 128), F32)]
        cmat = jnp.transpose(jnp.concatenate(padded, axis=0))[0:rows]
        terms = [jnp.take_along_axis(cmat, base + s, axis=1) for s in range(6)]
        polys = (
            terms[0] + x * (terms[1] + x * terms[3]),
            terms[2] + x * terms[4],
            terms[5],
        )
        first = jnp.concatenate(pieces[:2], axis=0)
        second = jnp.concatenate(pieces[2:], axis=0)
        return polys, first, second, which

    totals = [jnp.zeros((rows, 128), F32) for _ in range(bands)]
    for start in range(0, groups, 2):
        members = [slots[g * GROUP : (g + 1) * GROUP] for g in (start, start + 1)]
        chosen = [select(m) for m in members]
        parts = [split(image) for image, _, _ in chosen]
        both = jnp.concatenate([p[0] for p in parts] + [p[1] for p in parts], axis=0)
        filt = 0
        for degree in DEGREES:
            count = degree + 1
            for j0 in range(0, count, 2):
                js = range(j0, min(j0 + 2, count))
                lanes = slice((filt + j0) * 128, (filt + js[-1] + 1) * 128)
                wide = jnp.dot(both, dh_ref[:, lanes], preferred_element_type=F32)
                conv = (
                    wide[: 2 * ext]
                    + wide[2 * ext :]
                    + jnp.dot(both[: 2 * ext], dl_ref[:, lanes], preferred_element_type=F32)
                )
                for j in js:
                    part = conv[:, (j - j0) * 128 : (j - j0 + 1) * 128]
                    high, low = split(jnp.concatenate([part[:ext], part[ext:]], axis=1))
                    at = (filt + j) * 3 * ext
                    stack[at : at + ext] = high
                    stack[at + ext : at + 2 * ext] = low
                    stack[at + 2 * ext : at + 3 * ext] = high
            filt += count
        pair = [gather(m, *c[1:]) for m, c in zip(members, chosen)]
        poly0, poly1, poly2 = [
            jnp.concatenate([pair[0][0][k], pair[1][0][k]], axis=1) for k in range(3)
        ]
        model = jnp.zeros((rows, 256), F32)
        basis_start = 0
        filt = 0
        for degree in DEGREES:
            count = degree + 1
            index = {}
            k = basis_start
            for i in range(count):
                for j in range(count - i):
                    index[i, j] = k
                    k += 1
            for j in range(count):
                at = (filt + j) * 3 * ext
                rowed = jnp.dot(
                    tab_ref[filt * rows : (filt + count - j) * rows],
                    stack[at : at + 3 * ext],
                    preferred_element_type=F32,
                )
                for i in range(count - j):
                    n = index[i, j]
                    spatial = poly0[n : n + 1] + y * poly1[n : n + 1] + yy * poly2[n : n + 1]
                    model = model + spatial * rowed[i * rows : (i + 1) * rows]
            basis_start = k
            filt += count
        for g in range(2):
            _, first, second, which = pair[g]
            part = first - second * model[:, g * 128 : (g + 1) * 128]
            which = jnp.broadcast_to(which, (rows, 128))
            for b in range(bands):
                totals[b] = totals[b] + jnp.where(which == float(b), part, 0.0)
    for b in range(bands):
        folded = totals[b] + pltpu.roll(totals[b], 64, 1)
        out_ref[b] = (folded + pltpu.roll(folded, 96, 1))[:, 0:cols]


def swaps(count, start):
    pairs = [(i, i + 1) for i in range(start, count - 1, 2)]
    return pairs + [(j, i) for i, j in pairs]


def stay(array):
    return pltpu.with_memory_space_constraint(array, pltpu.HBM)


def per_device(template, science, variance, coeffs, visit_weight, band, footprint):
    visits, quads = lax.axis_size("visit"), lax.axis_size("quad")
    chips = visits // 2
    bands, rows, cols = template.shape
    ext = rows + 2 * EDGE
    short = rows // 2
    vmem = pl.BlockSpec(memory_space=pltpu.VMEM)
    hbm = pl.BlockSpec(memory_space=pltpu.HBM)
    params = pltpu.CompilerParams(vmem_limit_bytes=24 * 1024 * 1024)
    struct = jax.ShapeDtypeStruct

    def call(kernel, outs, ins, scratch=()):
        return pl.pallas_call(
            kernel,
            out_shape=outs,
            in_specs=ins,
            out_specs=jax.tree.map(lambda _: vmem, outs),
            scratch_shapes=scratch,
            compiler_params=params,
        )

    turned = jnp.transpose(coeffs, (2, 0, 1))
    sources = [stay(array) for array in (template, science, variance, turned, footprint)]
    strip = struct((-(-bands // GROUP), EDGE, 128), F32)
    first, second, wide, *loaded = call(
        functools.partial(load_kernel, len(sources)),
        [strip, strip, struct((bands, rows, 128), F32)]
        + [struct(a.shape, a.dtype) for a in sources[1:]],
        [hbm] * 5,
        [pltpu.VMEM(template.shape, F32), pltpu.SemaphoreType.DMA((5,))],
    )(*sources)
    halo_a = lax.ppermute(first, "quad", [(i, (i + 1) % quads) for i in range(quads)])
    halo_b = lax.ppermute(second, "quad", [((i + 1) % quads, i) for i in range(quads)])
    height = chips * short + 8
    mine, away = call(
        functools.partial(pack_kernel, visits, cols),
        [struct((height, 128), F32)] * 2,
        [vmem] * 4 + [pl.BlockSpec(memory_space=pltpu.SMEM)] * 2,
        [pltpu.VMEM((visits, short, 128), F32)],
    )(*loaded, visit_weight, band)
    got = lax.ppermute(away, "visit", swaps(visits, 0))
    own, to_core, to_chips = call(
        functools.partial(edge_kernel, cols, quads),
        [struct((bands, ext, 128), F32)] + [struct((ext // 2, 128), F32)] * 2,
        [vmem] * 3,
    )(wide, halo_a, halo_b)
    edge = lax.ppermute(to_core, "visit", swaps(visits, 0))
    steps = sorted({c ^ (c + 1) for c in range(chips - 1)})
    outgoing = call(
        functools.partial(merge_kernel, rows, steps),
        [
            struct((rows + 8 + (ext // 2 if m in steps else 0), 128), F32)
            for m in range(1, chips)
        ],
        [vmem] * 3,
    )(mine, got, to_chips)
    incoming = [
        lax.ppermute(array, "visit", [(i, i ^ (2 * m + 1)) for i in range(visits)])
        for m, array in enumerate(outgoing, 1)
    ]
    tables = [
        stay(jnp.asarray(array)) for array in (row_weights(rows),) + column_weights(cols, 64)
    ]
    tables = call(
        table_kernel,
        [struct(a.shape, a.dtype) for a in tables],
        [vmem] + [hbm] * 3,
        [pltpu.SemaphoreType.DMA((3,))],
    )(outgoing[0], *tables)
    return call(
        functools.partial(model_kernel, visits, quads, steps),
        struct((bands, rows, cols), F32),
        [vmem] * (7 + chips - 1),
        [pltpu.VMEM((bands, ext, 128), F32), pltpu.VMEM((12 * 3 * ext, 256), BF16)],
    )(mine, got, own, edge, *tables, *incoming)


def solution(mesh):
    placed = (
        P(None, "quad", "visit"),
        P("visit", "quad", None),
        P("visit", "quad", None),
        P("visit", None, None),
        P("visit"),
        P("visit"),
        P("visit", "quad", None),
    )
    return jax.shard_map(
        per_device, mesh=mesh, in_specs=placed, out_specs=P(None, "quad", "visit"), check_vma=False
    )
```
